512 devices in a mesh: seq: 64 (over z_lo, y, core), chan: 8 (over z_hi, x).
Axes of the slice: x: 4, y: 4, z: 16 (z_hi: 2, z_lo: 8; z = z_hi * 8 + z_lo), core: 2. Of those that a mesh axis runs over, the one named last changes fastest.
Arguments:
- inputs: bfloat16 [8192, 8192], P('seq', 'chan'), may hold values from -256 to 256
- gating: bfloat16 [8192, 8192], P('seq', 'chan'), may hold values from -6 to 6
- long_filter: bfloat16 [513, 8192], P(None, 'chan'), may hold values from -0.25 to 0.25
- skip_scale: float32 [8192], P('chan'), may hold values from 0.5 to 1.5
Outputs:
- gated: bfloat16 [8192, 8192], P('seq', 'chan')
The draws below stay inside these ranges and needn't reach their ends.
All inputs are finite; a program needn't handle non-finite values.
Results may differ from the reference program's by a relative error of at most 0.0049.
Values may be sent and summed in bfloat16 or wider, within the bound.
A program may use at most 64 MiB of HBM per device.

```python
import math
import jax
import jax.numpy as jnp
from jax import lax

D = 8192
FLEN = 513
TOKENS = 8192


def draw_inputs(key, part):
    first_key, second_key, third_key = jax.random.split(jax.random.fold_in(key, 11), 3)
    chan_pos = jnp.arange(D, dtype=jnp.float32) / max(D - 1, 1)
    rough = jnp.exp(jax.random.uniform(second_key, (1, D), jnp.float32, math.log(0.5), math.log(2.0)))
    row_scale = jnp.exp(jax.random.uniform(third_key, (TOKENS, 1), jnp.float32, 0.0, math.log(10.0)))
    column = jnp.power(10.0, 0.5 * chan_pos)[None, :]
    base = jax.random.normal(first_key, (TOKENS, D), jnp.float32)
    return jnp.clip(base * column * rough * row_scale, -256.0, 256.0).astype(jnp.bfloat16)


def shard_levels(rng, dims, pieces, least, high):
    level = 1.0
    for position, blocks in pieces:
        heights = jax.random.uniform(jax.random.fold_in(jax.random.fold_in(rng, 6), position), (blocks,), jnp.float32, least / len(pieces), high / len(pieces))
        level = level * jnp.repeat(jnp.exp(heights), dims[position] // blocks).reshape((-1,) + (1,) * (len(dims) - 1 - position))
    return level


def centred(own_key, extent, scale, reach, cuts=(), kind=jnp.bfloat16):
    factor_of = shard_levels(own_key, extent, cuts, -0.22, 0.18) if cuts else 1.0
    drawn = jax.random.normal(own_key, extent, jnp.float32) * scale * factor_of
    return jnp.minimum(jnp.maximum(drawn, -reach), reach).astype(kind)


def setup_inputs(seed: int = 0) -> dict:
    key_of = jax.random.split(jax.random.key(seed), 5)
    inputs = draw_inputs(jax.random.fold_in(key_of[4], 71), 0)
    gating = centred(key_of[1], (TOKENS, D), 1.0, 6.0, ((0, 64), (1, 8)))
    long_filter = centred(key_of[2], (FLEN, D), FLEN ** -0.5, 0.25, ((1, 8),))
    skip_scale = jnp.clip(0.5 + 1.0 * jax.random.uniform(key_of[3], (D,), jnp.float32) ** shard_levels(key_of[3], (D,), ((0, 8),), -0.2, 0.2), 0.5, 1.5)
    return dict(inputs=inputs, gating=gating, long_filter=long_filter, skip_scale=skip_scale)


def reference(inputs, gating, long_filter, skip_scale):
    values = inputs.astype(jnp.float32)
    mean_square = lax.optimization_barrier(jnp.mean(values * values, axis=1, keepdims=True))
    normed = (values * lax.rsqrt(mean_square + 1e-06)).astype(jnp.bfloat16)
    seq_length = normed.shape[0]
    tap_count = long_filter.shape[0]
    fft_size = 1 << (seq_length + tap_count - 1).bit_length()
    chan_block = min(D, 256)

    def block_conv(start):
        signal = lax.dynamic_slice_in_dim(normed, start, chan_block, 1).astype(jnp.float32)
        kernel = lax.dynamic_slice_in_dim(long_filter, start, chan_block, 1).astype(jnp.float32)
        spectrum = jnp.fft.rfft(signal, n=fft_size, axis=0) * jnp.fft.rfft(kernel, n=fft_size, axis=0)
        return jnp.fft.irfft(spectrum, n=fft_size, axis=0)[:seq_length].astype(jnp.float32)
    starts = jnp.arange(0, D, chan_block, dtype=jnp.int32)
    blocks = lax.map(block_conv, starts)
    convolved = jnp.transpose(blocks, (1, 0, 2)).reshape(seq_length, D)
    mixed = gating.astype(jnp.float32) * (convolved + skip_scale[None, :] * normed.astype(jnp.float32))
    return mixed.astype(jnp.bfloat16)
```

```python
import math

import jax
import jax.numpy as jnp
import numpy as np
from jax import lax
from jax.experimental import pallas as pl
from jax.experimental.pallas import tpu as pltpu
from jax.sharding import PartitionSpec as P

D = 8192
MESH = pl.DeviceIdType.MESH
B = 128
LAGS = 4
RING = 128
FAR = 32
CW = 256
CHUNKS = 4
ROWS = B // CHUNKS


def split(value):
    hi = value.astype(jnp.bfloat16)
    return hi, (value - hi.astype(jnp.float32)).astype(jnp.bfloat16)


def tables():
    bins = np.concatenate([np.arange(0, B, 2), np.arange(1, B, 2)])
    angle = np.pi * np.outer(2 * bins + 1, np.arange(B)) / (2 * B)
    forward = np.concatenate([np.cos(angle), -np.sin(angle)], 0)
    inverse = forward.T / B

    def halves(table):
        table = table.astype(np.float32)
        hi = table.astype(jnp.bfloat16)
        lo = (table - hi.astype(np.float32)).astype(jnp.bfloat16)
        return np.concatenate([hi, lo], 1)

    return forward.astype(np.float32), halves(forward), halves(inverse)


def kernel(
    x_hbm,
    gate_hbm,
    taps_hbm,
    skip_hbm,
    ftab_hbm,
    fcat_hbm,
    icat_hbm,
    out,
    xv,
    gate,
    taps,
    skip,
    ftab,
    fcat,
    icat,
    halo,
    spec,
    fs,
    part,
    xpart,
    zsum,
    zpart,
    total,
    ytotal,
    load_sem,
    own_send,
    fwd_send,
    mate_send,
    halo_recv,
    x_send,
    x_recv,
    z_send,
    z_recv,
    y_send,
    y_recv,
):
    seq, chan = lax.axis_index("seq"), lax.axis_index("chan")
    half, col = lax.div(chan, 4), lax.rem(chan, 4)
    place = half * 64 + seq
    odd = lax.rem(place, 2) == 1

    def at(shift):
        spot = lax.rem(place + (shift + RING), RING)
        return (lax.rem(spot, 64), lax.div(spot, 64) * 4 + col)

    def beside(shift):
        return (seq, half * 4 + lax.rem(col + shift, 4))

    loads = [
        pltpu.make_async_copy(src, dst, load_sem.at[n])
        for n, (src, dst) in enumerate(
            [
                (x_hbm, xv),
                (fcat_hbm, fcat),
                (taps_hbm, taps),
                (skip_hbm, skip),
                (ftab_hbm, ftab),
                (icat_hbm, icat),
                (gate_hbm, gate),
            ]
        )
    ]
    for load in loads:
        load.start()

    barrier = pltpu.get_barrier_semaphore()
    peers = [beside(d) for d in (1, 2, 3)]
    peers += [at(d) for k in (1, 2, 3, 4, FAR) for d in (k, -k)]
    for peer in peers:
        pl.semaphore_signal(barrier, inc=1, device_id=peer, device_id_type=MESH)
    pl.semaphore_wait(barrier, len(peers))

    def remote(src, dst, send, recv, device):
        return pltpu.make_async_remote_copy(
            src_ref=src,
            dst_ref=dst,
            send_sem=send,
            recv_sem=recv,
            device_id=device,
            device_id_type=MESH,
        )

    def piece(n):
        return pl.ds(n * ROWS, ROWS)

    mate = lax.rem(place, 2) * -2 + 1

    def to_next(src, slot, n, send):
        return remote(
            src.at[piece(n)], halo.at[slot, piece(n)], send.at[n], halo_recv.at[slot, n], at(2)
        )

    def to_mate(src, slot, n):
        return remote(
            src.at[piece(n)],
            halo.at[slot, piece(n)],
            mate_send.at[slot // 2, n],
            halo_recv.at[slot, n],
            at(mate),
        )

    own = [to_next(x_hbm, 1, n, own_send) for n in range(CHUNKS)]
    for copy in own:
        copy.start()

    @pl.when(jnp.logical_not(odd))
    def _():
        for n in range(CHUNKS):
            to_mate(x_hbm, 0, n).start()

    loads[0].wait()
    gram = lax.dot_general(
        xv[...], xv[...], (((1,), (1,)), ((), ())), preferred_element_type=jnp.float32
    )
    diagonal = lax.broadcasted_iota(jnp.int32, (B, B), 0) == lax.broadcasted_iota(
        jnp.int32, (B, B), 1
    )
    part[...] = jnp.sum(jnp.where(diagonal, gram, 0.0), axis=0, keepdims=True)
    xs = [
        remote(part, xpart.at[d - 1], x_send.at[d - 1], x_recv.at[d - 1], beside(d))
        for d in (1, 2, 3)
    ]
    for copy in xs:
        copy.start()

    for load in loads[1:]:
        load.wait()

    def filter_spectra(step, carry):
        cols = pl.ds(pl.multiple_of(step * CW, CW), CW)
        last_re = last_im = None
        for lag in range(LAGS + 1):
            if lag < LAGS:
                block = taps[lag * B : (lag + 1) * B, cols]
                here = jnp.dot(
                    fcat[...],
                    jnp.concatenate([block, block], 0),
                    preferred_element_type=jnp.float32,
                )
                re, im = here[:B], here[B:]
                if lag == 0:
                    full_re, full_im = re + skip[:, cols], im
                else:
                    full_re, full_im = re, im
            else:
                full_re = jnp.broadcast_to(taps[LAGS * B : LAGS * B + 1, cols].astype(jnp.float32), (B, CW))
                full_im = None
            if last_re is not None:
                h = B // 2
                full_re = jnp.concatenate(
                    [full_re[:h] - last_im[:h], full_re[h:] + last_im[h:]], 0
                )
                if full_im is None:
                    full_im = jnp.concatenate([last_re[:h], -last_re[h:]], 0)
                else:
                    full_im = jnp.concatenate(
                        [full_im[:h] + last_re[:h], full_im[h:] - last_re[h:]], 0
                    )
            spec[lag, :B, cols] = full_re
            spec[lag, B:, cols] = full_im
            if lag < LAGS:
                last_re, last_im = re, im
        return carry

    steps = xv.shape[1] // CW
    lax.fori_loop(0, steps // 2, filter_spectra, 0)

    for copy in xs:
        copy.wait_recv()
    zsum[...] = part[...] + xpart[0] + xpart[1] + xpart[2]
    first_leg = remote(zsum, zpart.at[0], z_send.at[0], z_recv.at[0], at(FAR))
    first_leg.start()

    lax.fori_loop(steps // 2, steps, filter_spectra, 0)

    def forward(n):
        own[n].wait_recv()
        to_next(halo.at[1], 3, n, fwd_send).start()

        @pl.when(odd)
        def _():
            to_mate(halo.at[1], 0, n).start()

        @pl.when(jnp.logical_not(odd))
        def _():
            to_mate(halo.at[1], 2, n).start()

    forward(0)
    forward(1)
    first_leg.wait_recv()
    second_leg = remote(zpart.at[0], zpart.at[1], z_send.at[1], z_recv.at[1], at(FAR))
    second_leg.start()
    forward(2)
    forward(3)
    second_leg.wait_recv()
    total[...] = zsum[...] + zpart[1]
    ys = [
        remote(total, ytotal.at[k - 1], y_send.at[k - 1], y_recv.at[k - 1], at(k))
        for k in range(1, LAGS + 1)
    ]
    for copy in ys:
        copy.start()

    def scaled(lag, sums):
        scale = lax.rsqrt(sums * (1.0 / D) + 1e-06)
        scale = jnp.where(seq >= lag, scale, 0.0)
        hi, lo = split(ftab[...] * scale)
        fs[lag, :, :B] = hi
        fs[lag, :, B:] = lo

    scaled(0, total[...])

    fwd = [to_next(halo.at[1], 3, n, fwd_send) for n in range(CHUNKS)]
    for n in range(CHUNKS):
        fwd[n].wait_recv()

        @pl.when(odd)
        def _():
            to_mate(halo.at[3], 2, n).start()

    for k in range(1, LAGS + 1):
        ys[k - 1].wait_recv()
        scaled(k, ytotal[k - 1])
    for n in range(CHUNKS):
        to_mate(halo.at[1], 0, n).wait_recv()
        to_mate(halo.at[1], 2, n).wait_recv()

    def convolve(step, carry):
        cols = pl.ds(pl.multiple_of(step * CW, CW), CW)
        acc_re = acc_im = None
        for lag in range(LAGS + 1):
            block = xv[:, cols] if lag == 0 else halo[lag - 1, :, cols]
            here = jnp.dot(
                fs[lag],
                jnp.concatenate([block, block], 0),
                preferred_element_type=jnp.float32,
            )
            re, im = here[:B], here[B:]
            sre, sim = spec[lag, :B, cols], spec[lag, B:, cols]
            pre, pim = re * sre - im * sim, re * sim + im * sre
            acc_re = pre if lag == 0 else acc_re + pre
            acc_im = pim if lag == 0 else acc_im + pim
        hi, lo = split(jnp.concatenate([acc_re, acc_im], 0))
        ihi, ilo = icat[:, : 2 * B], icat[:, 2 * B :]
        result = (
            jnp.dot(ihi, hi, preferred_element_type=jnp.float32)
            + jnp.dot(ihi, lo, preferred_element_type=jnp.float32)
            + jnp.dot(ilo, hi, preferred_element_type=jnp.float32)
        )
        out[:, cols] = (gate[:, cols].astype(jnp.float32) * result).astype(jnp.bfloat16)
        return carry

    lax.fori_loop(0, steps, convolve, 0)

    for copy in own + fwd + xs + [first_leg, second_leg] + ys:
        copy.wait_send()
    for n in range(CHUNKS):
        to_mate(halo.at[1], 0, n).wait_send()
        to_mate(halo.at[1], 2, n).wait_send()


def on_device(inputs, gating, long_filter, skip_scale):
    rows, channels = inputs.shape
    bf16, f32 = jnp.bfloat16, jnp.float32
    ftab, fcat, icat = tables()
    dma = pltpu.SemaphoreType.DMA
    return pl.pallas_call(
        kernel,
        out_shape=jax.ShapeDtypeStruct((rows, channels), bf16),
        in_specs=[pl.BlockSpec(memory_space=pltpu.HBM)] * 7,
        out_specs=pl.BlockSpec(memory_space=pltpu.VMEM),
        scratch_shapes=[
            pltpu.VMEM((rows, channels), bf16),
            pltpu.VMEM((rows, channels), bf16),
            pltpu.VMEM(long_filter.shape, bf16),
            pltpu.VMEM((1, channels), f32),
            pltpu.VMEM(ftab.shape, f32),
            pltpu.VMEM(fcat.shape, bf16),
            pltpu.VMEM(icat.shape, bf16),
            pltpu.VMEM((LAGS, rows, channels), bf16),
            pltpu.VMEM((LAGS + 1, 2 * B, channels), f32),
            pltpu.VMEM((LAGS + 1, 2 * B, 2 * B), bf16),
            pltpu.VMEM((1, B), f32),
            pltpu.VMEM((3, 1, B), f32),
            pltpu.VMEM((1, B), f32),
            pltpu.VMEM((2, 1, B), f32),
            pltpu.VMEM((1, B), f32),
            pltpu.VMEM((LAGS, 1, B), f32),
            dma((7,)),
            dma((CHUNKS,)),
            dma((CHUNKS,)),
            dma((2, CHUNKS)),
            dma((LAGS, CHUNKS)),
            dma((3,)),
            dma((3,)),
            dma((2,)),
            dma((2,)),
            dma((LAGS,)),
            dma((LAGS,)),
        ],
        compiler_params=pltpu.CompilerParams(
            collective_id=0, has_side_effects=True, vmem_limit_bytes=60 * 1024 * 1024
        ),
    )(inputs, gating, long_filter, skip_scale[None, :], ftab, fcat, icat)


def solution(mesh):
    in_specs = (P("seq", "chan"), P("seq", "chan"), P(None, "chan"), P("chan"))
    return jax.shard_map(
        on_device, mesh=mesh, in_specs=in_specs, out_specs=P("seq", "chan"), check_vma=False
    )
```

```python
import functools

import jax
import jax.numpy as jnp
import numpy as np
from jax import lax
from jax.experimental import pallas as pl
from jax.experimental.pallas import tpu as pltpu
from jax.sharding import PartitionSpec as P

D = 8192
MESH = pl.DeviceIdType.MESH
B = 128
LAGS = 4
CW = 256
CHUNKS = 4
ROWS = B // CHUNKS


def split(value):
    hi = value.astype(jnp.bfloat16)
    return hi, (value - hi.astype(jnp.float32)).astype(jnp.bfloat16)


def tables():
    bins = np.concatenate([np.arange(0, B, 2), np.arange(1, B, 2)])
    angle = np.pi * np.outer(2 * bins + 1, np.arange(B)) / (2 * B)
    forward = np.concatenate([np.cos(angle), -np.sin(angle)], 0)
    inverse = forward.T / B

    def halves(table):
        table = table.astype(np.float32)
        hi = table.astype(jnp.bfloat16)
        lo = (table - hi.astype(np.float32)).astype(jnp.bfloat16)
        return np.concatenate([hi, lo], 1)

    return forward.astype(np.float32), halves(forward), halves(inverse)


def kernel(
    x_hbm,
    gate_hbm,
    taps_hbm,
    skip_hbm,
    ftab_hbm,
    fcat_hbm,
    icat_hbm,
    out,
    xv,
    gate,
    taps,
    skip,
    ftab,
    fcat,
    icat,
    halo,
    spec,
    acc,
    part,
    xpart,
    xsum,
    near,
    away,
    load_sem,
    own_send,
    fwd_send,
    mate_send,
    halo_recv,
    x_send,
    x_recv,
    near_send,
    near_recv,
    away_send,
    away_recv,
    ready,
):
    seq, chan = lax.axis_index("seq"), lax.axis_index("chan")
    count = lax.axis_size("seq")
    half, col = lax.div(chan, 4), lax.rem(chan, 4)
    upper = half == 1
    odd = lax.rem(seq, 2) == 1
    even = jnp.logical_not(odd)
    lags = range(1, LAGS + 1)
    spans = range(LAGS + 1)

    def ahead(k):
        return (seq + k, chan)

    def across(k):
        return (seq + k, (1 - half) * 4 + col)

    def beside(shift):
        return (seq, half * 4 + lax.rem(col + shift, 4))

    def has(k):
        return jnp.logical_and(seq + k >= 0, seq + k < count)

    def signal(sem, device):
        pl.semaphore_signal(sem, inc=1, device_id=device, device_id_type=MESH)

    loads = [
        pltpu.make_async_copy(src, dst, load_sem.at[n])
        for n, (src, dst) in enumerate(
            [
                (x_hbm, xv),
                (fcat_hbm, fcat),
                (taps_hbm, taps),
                (skip_hbm, skip),
                (ftab_hbm, ftab),
                (icat_hbm, icat),
                (gate_hbm, gate),
            ]
        )
    ]

    barrier = pltpu.get_barrier_semaphore()
    for k in lags:
        pl.when(has(-k))(functools.partial(signal, barrier, ahead(-k)))
    pl.when(even)(functools.partial(signal, barrier, ahead(1)))
    for shift in (1, 2, 3):
        signal(barrier, beside(shift))

    @pl.when(jnp.logical_not(upper))
    def _():
        for k in range(-LAGS, LAGS + 1):
            pl.when(has(k))(functools.partial(signal, barrier, across(k)))

    for load in loads:
        load.start()

    before, after = jnp.minimum(seq, LAGS), jnp.minimum(count - 1 - seq, LAGS)
    pl.semaphore_wait(barrier, 3 + after + lax.rem(seq, 2) + half * (before + after + 1))

    @pl.when(upper)
    def _():
        for k in spans:
            pl.when(has(-k))(functools.partial(signal, ready, across(-k)))

    def remote(src, dst, send, recv, device):
        return pltpu.make_async_remote_copy(
            src_ref=src,
            dst_ref=dst,
            send_sem=send,
            recv_sem=recv,
            device_id=device,
            device_id_type=MESH,
        )

    def piece(n):
        return pl.ds(n * ROWS, ROWS)

    def to_next(src, slot, n, send):
        return remote(
            src.at[piece(n)], halo.at[slot, piece(n)], send.at[n], halo_recv.at[slot, n], ahead(2)
        )

    def to_mate(src, slot, n):
        return remote(
            src.at[piece(n)],
            halo.at[slot, piece(n)],
            mate_send.at[slot // 2, n],
            halo_recv.at[slot, n],
            ahead(1 - 2 * lax.rem(seq, 2)),
        )

    pieces = range(CHUNKS)
    own = [to_next(x_hbm, 1, n, own_send) for n in pieces]
    onward = [to_next(halo.at[1], 3, n, fwd_send) for n in pieces]
    even_first = [to_mate(x_hbm, 0, n) for n in pieces]
    even_second = [to_mate(halo.at[1], 2, n) for n in pieces]
    odd_first = [to_mate(halo.at[1], 0, n) for n in pieces]
    odd_second = [to_mate(halo.at[3], 2, n) for n in pieces]

    def each(copies, act):
        for copy in copies:
            act(copy)

    @pl.when(has(2))
    def _():
        each(own, lambda copy: copy.start())

    loads[0].wait()
    gram = lax.dot_general(
        xv[...], xv[...], (((1,), (1,)), ((), ())), preferred_element_type=jnp.float32
    )
    diagonal = lax.broadcasted_iota(jnp.int32, (B, B), 0) == lax.broadcasted_iota(
        jnp.int32, (B, B), 1
    )
    part[...] = jnp.sum(jnp.where(diagonal, gram, 0.0), axis=0, keepdims=True)
    xs = [
        remote(part, xpart.at[d - 1], x_send.at[d - 1], x_recv.at[d - 1], beside(d))
        for d in (1, 2, 3)
    ]
    each(xs, lambda copy: copy.start())

    @pl.when(even)
    def _():
        each(even_first, lambda copy: copy.start())

    for k in lags:

        @pl.when(seq < k)
        def _():
            halo[k - 1] = jnp.zeros(halo.shape[1:], halo.dtype)

    each(loads[1:4], lambda copy: copy.wait())

    def filter_spectra(step, carry):
        cols = pl.ds(pl.multiple_of(step * CW, CW), CW)
        last_re = last_im = None
        for lag in spans:
            if lag < LAGS:
                block = taps[lag * B : (lag + 1) * B, cols]
                here = jnp.dot(
                    fcat[...],
                    jnp.concatenate([block, block], 0),
                    preferred_element_type=jnp.float32,
                )
                re, im = here[:B], here[B:]
                full_re, full_im = (re + skip[:, cols] if lag == 0 else re), im
            else:
                tap = taps[LAGS * B : LAGS * B + 1, cols].astype(jnp.float32)
                full_re, full_im = jnp.broadcast_to(tap, (B, CW)), jnp.zeros((B, CW), jnp.float32)
            if last_re is not None:
                h = B // 2
                turned_re = jnp.concatenate([-last_im[:h], last_im[h:]], 0)
                turned_im = jnp.concatenate([last_re[:h], -last_re[h:]], 0)
                full_re, full_im = full_re + turned_re, full_im + turned_im
            spec[lag, :B, cols] = full_re
            spec[lag, B:, cols] = full_im
            if lag < LAGS:
                last_re, last_im = re, im
        return carry

    steps = xv.shape[1] // CW
    lax.fori_loop(0, steps // 2, filter_spectra, 0)

    each(xs, lambda copy: copy.wait_recv())
    xsum[...] = part[...] + xpart[0] + xpart[1] + xpart[2]
    nears = [
        remote(xsum, near.at[k - 1], near_send.at[k - 1], near_recv.at[k - 1], ahead(k))
        for k in lags
    ]
    aways = [
        remote(xsum, away.at[k], away_send.at[k], away_recv.at[k], across(k)) for k in spans
    ]

    def send_away():
        for k in spans:
            pl.when(has(k))(lambda copy=aways[k]: copy.start())

    pl.when(upper)(send_away)
    for k in lags:
        pl.when(has(k))(lambda copy=nears[k - 1]: copy.start())

    lax.fori_loop(steps // 2, steps, filter_spectra, 0)

    @pl.when(has(-2))
    def _():
        for n in pieces:
            own[n].wait_recv()
            pl.when(has(2))(lambda n=n: onward[n].start())
            pl.when(odd)(lambda n=n: odd_first[n].start())
            pl.when(even)(lambda n=n: even_second[n].start())

    @pl.when(jnp.logical_not(upper))
    def _():
        pl.semaphore_wait(ready, after + 1)
        send_away()

    @pl.when(has(-4))
    def _():
        for n in pieces:
            onward[n].wait_recv()
            pl.when(odd)(lambda n=n: odd_second[n].start())

    each(loads[4:], lambda copy: copy.wait())

    def scaled(lag):
        if lag == 0:
            sums = xsum[...] + away[0]
        else:
            sums = near[lag - 1] + away[lag]
        scale = lax.rsqrt(sums * (1.0 / D) + 1e-06)
        if lag:
            scale = jnp.where(seq >= lag, scale, 0.0)
        return jnp.concatenate(split(ftab[...] * scale), 1)

    def arrived(lag):
        if lag in (1, 3):
            each(odd_first if lag == 1 else odd_second, lambda copy: copy.wait_recv())
        nears[lag - 1].wait_recv()
        aways[lag].wait_recv()

    for lag in spans:
        if lag == 0:
            aways[0].wait_recv()
        else:
            pl.when(seq >= lag)(functools.partial(arrived, lag))
        table = scaled(lag)

        def convolve(step, carry, lag=lag, table=table):
            cols = pl.ds(pl.multiple_of(step * CW, CW), CW)
            block = xv[:, cols] if lag == 0 else halo[lag - 1, :, cols]
            here = jnp.dot(
                table, jnp.concatenate([block, block], 0), preferred_element_type=jnp.float32
            )
            re, im = here[:B], here[B:]
            sre, sim = spec[lag, :B, cols], spec[lag, B:, cols]
            new_re, new_im = re * sre - im * sim, re * sim + im * sre
            if lag:
                new_re, new_im = new_re + acc[:B, cols], new_im + acc[B:, cols]
            if lag < LAGS:
                acc[:B, cols] = new_re
                acc[B:, cols] = new_im
                return carry
            hi, lo = split(jnp.concatenate([new_re, new_im], 0))
            ihi, ilo = icat[:, : 2 * B], icat[:, 2 * B :]
            result = (
                jnp.dot(ihi, hi, preferred_element_type=jnp.float32)
                + jnp.dot(ihi, lo, preferred_element_type=jnp.float32)
                + jnp.dot(ilo, hi, preferred_element_type=jnp.float32)
            )
            out[:, cols] = (gate[:, cols].astype(jnp.float32) * result).astype(jnp.bfloat16)
            return carry

        lax.fori_loop(0, steps, convolve, 0)

    each(xs, lambda copy: copy.wait_send())
    for k in spans:
        pl.when(has(k))(lambda copy=aways[k]: copy.wait_send())
    for k in lags:
        pl.when(has(k))(lambda copy=nears[k - 1]: copy.wait_send())

    def sent(copies):
        each(copies, lambda copy: copy.wait_send())

    pl.when(has(2))(lambda: sent(own))
    pl.when(jnp.logical_and(has(2), has(-2)))(lambda: sent(onward))
    pl.when(even)(lambda: sent(even_first))
    pl.when(jnp.logical_and(even, has(-2)))(lambda: sent(even_second))
    pl.when(jnp.logical_and(odd, has(-2)))(lambda: sent(odd_first))
    pl.when(jnp.logical_and(odd, has(-4)))(lambda: sent(odd_second))


def on_device(inputs, gating, long_filter, skip_scale):
    rows, channels = inputs.shape
    bf16, f32 = jnp.bfloat16, jnp.float32
    ftab, fcat, icat = tables()
    dma = pltpu.SemaphoreType.DMA
    return pl.pallas_call(
        kernel,
        out_shape=jax.ShapeDtypeStruct((rows, channels), bf16),
        in_specs=[pl.BlockSpec(memory_space=pltpu.HBM)] * 7,
        out_specs=pl.BlockSpec(memory_space=pltpu.VMEM),
        scratch_shapes=[
            pltpu.VMEM((rows, channels), bf16),
            pltpu.VMEM((rows, channels), bf16),
            pltpu.VMEM(long_filter.shape, bf16),
            pltpu.VMEM((1, channels), f32),
            pltpu.VMEM(ftab.shape, f32),
            pltpu.VMEM(fcat.shape, bf16),
            pltpu.VMEM(icat.shape, bf16),
            pltpu.VMEM((LAGS, rows, channels), bf16),
            pltpu.VMEM((LAGS + 1, 2 * B, channels), f32),
            pltpu.VMEM((2 * B, channels), f32),
            pltpu.VMEM((1, B), f32),
            pltpu.VMEM((3, 1, B), f32),
            pltpu.VMEM((1, B), f32),
            pltpu.VMEM((LAGS, 1, B), f32),
            pltpu.VMEM((LAGS + 1, 1, B), f32),
            dma((7,)),
            dma((CHUNKS,)),
            dma((CHUNKS,)),
            dma((2, CHUNKS)),
            dma((LAGS, CHUNKS)),
            dma((3,)),
            dma((3,)),
            dma((LAGS,)),
            dma((LAGS,)),
            dma((LAGS + 1,)),
            dma((LAGS + 1,)),
            pltpu.SemaphoreType.REGULAR,
        ],
        compiler_params=pltpu.CompilerParams(
            collective_id=0, has_side_effects=True, vmem_limit_bytes=60 * 1024 * 1024
        ),
    )(inputs, gating, long_filter, skip_scale[None, :], ftab, fcat, icat)


def solution(mesh):
    in_specs = (P("seq", "chan"), P("seq", "chan"), P(None, "chan"), P("chan"))
    return jax.shard_map(
        on_device, mesh=mesh, in_specs=in_specs, out_specs=P("seq", "chan"), check_vma=False
    )
```

```python
import functools

import jax
import jax.numpy as jnp
import numpy as np
from jax import lax
from jax.experimental import pallas as pl
from jax.experimental.pallas import tpu as pltpu
from jax.sharding import PartitionSpec as P

D = 8192
MESH = pl.DeviceIdType.MESH
B = 128
LAGS = 4
CW = 256
WIDE = 512
CHUNKS = 4
ROWS = B // CHUNKS


def split(value):
    hi = value.astype(jnp.bfloat16)
    return hi, (value - hi.astype(jnp.float32)).astype(jnp.bfloat16)


def tables():
    bins = np.concatenate([np.arange(0, B, 2), np.arange(1, B, 2)])
    angle = np.pi * np.outer(2 * bins + 1, np.arange(B)) / (2 * B)
    forward = np.concatenate([np.cos(angle), -np.sin(angle)], 0)
    inverse = forward.T / B

    def halves(table):
        table = table.astype(np.float32)
        hi = table.astype(jnp.bfloat16)
        lo = (table - hi.astype(np.float32)).astype(jnp.bfloat16)
        return np.concatenate([hi, lo], 1)

    return forward.astype(np.float32), halves(forward), halves(inverse)


def kernel(
    x_hbm,
    gate_hbm,
    taps_hbm,
    skip_hbm,
    ftab_hbm,
    fcat_hbm,
    icat_hbm,
    out_hbm,
    xv,
    gate,
    taps,
    skip,
    ftab,
    fcat,
    icat,
    halo,
    spec,
    fs,
    out,
    part,
    xpart,
    xsum,
    near,
    away,
    load_sem,
    own_send,
    fwd_send,
    mate_send,
    halo_recv,
    x_send,
    x_recv,
    near_send,
    near_recv,
    away_send,
    away_recv,
    ready,
    go,
    out_sem,
):
    seq, chan = lax.axis_index("seq"), lax.axis_index("chan")
    count = lax.axis_size("seq")
    half, col = lax.div(chan, 4), lax.rem(chan, 4)
    upper = half == 1
    odd = lax.rem(seq, 2) == 1
    even = jnp.logical_not(odd)
    lags = range(1, LAGS + 1)
    spans = range(LAGS + 1)

    def ahead(k):
        return (seq + k, chan)

    def across(k):
        return (seq + k, (1 - half) * 4 + col)

    def beside(shift):
        return (seq, half * 4 + lax.rem(col + shift, 4))

    def has(k):
        return jnp.logical_and(seq + k >= 0, seq + k < count)

    def signal(sem, device):
        pl.semaphore_signal(sem, inc=1, device_id=device, device_id_type=MESH)

    loads = [
        pltpu.make_async_copy(src, dst, load_sem.at[n])
        for n, (src, dst) in enumerate(
            [
                (x_hbm, xv),
                (fcat_hbm, fcat),
                (taps_hbm, taps),
                (skip_hbm, skip),
                (ftab_hbm, ftab),
                (icat_hbm, icat),
                (gate_hbm, gate),
            ]
        )
    ]

    loads[0].start()
    barrier = pltpu.get_barrier_semaphore()
    for shift in (1, 2, 3):
        signal(barrier, beside(shift))
    for k in lags:
        pl.when(has(k))(functools.partial(signal, barrier, ahead(k)))

    @pl.when(jnp.logical_not(upper))
    def _():
        for k in range(-LAGS, LAGS + 1):
            pl.when(has(k))(functools.partial(signal, barrier, across(k)))

    for load in loads[1:]:
        load.start()

    loads[0].wait()
    gram = lax.dot_general(
        xv[...], xv[...], (((1,), (1,)), ((), ())), preferred_element_type=jnp.float32
    )
    diagonal = lax.broadcasted_iota(jnp.int32, (B, B), 0) == lax.broadcasted_iota(
        jnp.int32, (B, B), 1
    )
    part[...] = jnp.sum(jnp.where(diagonal, gram, 0.0), axis=0, keepdims=True)

    before, after = jnp.minimum(seq, LAGS), jnp.minimum(count - 1 - seq, LAGS)
    pl.semaphore_wait(barrier, 3 + before + half * (before + after + 1))

    def remote(src, dst, send, recv, device):
        return pltpu.make_async_remote_copy(
            src_ref=src,
            dst_ref=dst,
            send_sem=send,
            recv_sem=recv,
            device_id=device,
            device_id_type=MESH,
        )

    def piece(n):
        return pl.ds(n * ROWS, ROWS)

    def to_next(src, slot, n, send):
        return remote(
            src.at[piece(n)], halo.at[slot, piece(n)], send.at[n], halo_recv.at[slot, n], ahead(2)
        )

    def to_mate(src, slot, n):
        return remote(
            src.at[piece(n)],
            halo.at[slot, piece(n)],
            mate_send.at[slot // 2, n],
            halo_recv.at[slot, n],
            ahead(1 - 2 * lax.rem(seq, 2)),
        )

    pieces = range(CHUNKS)
    own = [to_next(x_hbm, 1, n, own_send) for n in pieces]
    onward = [to_next(halo.at[1], 3, n, fwd_send) for n in pieces]
    even_first = [to_mate(x_hbm, 0, n) for n in pieces]
    even_second = [to_mate(halo.at[1], 2, n) for n in pieces]
    odd_first = [to_mate(halo.at[1], 0, n) for n in pieces]
    odd_second = [to_mate(halo.at[3], 2, n) for n in pieces]

    def each(copies, act):
        for copy in copies:
            act(copy)

    xs = [
        remote(part, xpart.at[d - 1], x_send.at[d - 1], x_recv.at[d - 1], beside(d))
        for d in (1, 2, 3)
    ]
    each(xs, lambda copy: copy.start())

    for k in (2, 1, 3, 4):
        pl.when(has(-k))(functools.partial(signal, go.at[k - 1], ahead(-k)))

    @pl.when(upper)
    def _():
        for k in spans:
            pl.when(has(-k))(functools.partial(signal, ready, across(-k)))

    for k in lags:

        @pl.when(seq < k)
        def _():
            halo[k - 1] = jnp.zeros(halo.shape[1:], halo.dtype)

    each(loads[1:4], lambda copy: copy.wait())

    def filter_spectra(step, carry):
        cols = pl.ds(pl.multiple_of(step * CW, CW), CW)
        last_re = last_im = None
        for lag in spans:
            if lag < LAGS:
                block = taps[lag * B : (lag + 1) * B, cols]
                here = jnp.dot(
                    fcat[...],
                    jnp.concatenate([block, block], 0),
                    preferred_element_type=jnp.float32,
                )
                re, im = here[:B], here[B:]
                full_re, full_im = (re + skip[:, cols] if lag == 0 else re), im
            else:
                tap = taps[LAGS * B : LAGS * B + 1, cols].astype(jnp.float32)
                full_re, full_im = jnp.broadcast_to(tap, (B, CW)), jnp.zeros((B, CW), jnp.float32)
            if last_re is not None:
                h = B // 2
                turned_re = jnp.concatenate([-last_im[:h], last_im[h:]], 0)
                turned_im = jnp.concatenate([last_re[:h], -last_re[h:]], 0)
                full_re, full_im = full_re + turned_re, full_im + turned_im
            spec[lag, :B, cols] = full_re
            spec[lag, B:, cols] = full_im
            if lag < LAGS:
                last_re, last_im = re, im
        return carry

    steps = xv.shape[1] // CW
    lax.fori_loop(0, steps, filter_spectra, 0)

    @pl.when(has(2))
    def _():
        pl.semaphore_wait(go.at[1], 1)
        each(own, lambda copy: copy.start())

    @pl.when(has(1))
    def _():
        pl.semaphore_wait(go.at[0], 1)

        @pl.when(even)
        def _():
            each(even_first, lambda copy: copy.start())

    each(xs, lambda copy: copy.wait_recv())
    xsum[...] = part[...] + xpart[0] + xpart[1] + xpart[2]
    nears = [
        remote(xsum, near.at[k - 1], near_send.at[k - 1], near_recv.at[k - 1], ahead(k))
        for k in lags
    ]
    aways = [
        remote(xsum, away.at[k], away_send.at[k], away_recv.at[k], across(k)) for k in spans
    ]

    def send_away():
        for k in spans:
            pl.when(has(k))(lambda copy=aways[k]: copy.start())

    pl.when(upper)(send_away)
    for k in lags:

        @pl.when(has(k))
        def _():
            if k > 2:
                pl.semaphore_wait(go.at[k - 1], 1)
            nears[k - 1].start()

    @pl.when(has(-2))
    def _():
        for n in pieces:
            own[n].wait_recv()
            pl.when(has(2))(lambda n=n: onward[n].start())
            pl.when(odd)(lambda n=n: odd_first[n].start())
            pl.when(even)(lambda n=n: even_second[n].start())

    @pl.when(jnp.logical_not(upper))
    def _():
        pl.semaphore_wait(ready, after + 1)
        send_away()

    @pl.when(has(-4))
    def _():
        for n in pieces:
            onward[n].wait_recv()
            pl.when(odd)(lambda n=n: odd_second[n].start())

    each(loads[4:], lambda copy: copy.wait())

    def scaled(lag):
        if lag == 0:
            sums = xsum[...] + away[0]
        else:
            sums = near[lag - 1] + away[lag]
        scale = lax.rsqrt(sums * (1.0 / D) + 1e-06)
        if lag:
            scale = jnp.where(seq >= lag, scale, 0.0)
        hi, lo = split(ftab[...] * scale)
        fs[lag, :, :B] = hi
        fs[lag, :, B:] = lo

    def arrived(lag):
        if lag in (1, 3):
            each(odd_first if lag == 1 else odd_second, lambda copy: copy.wait_recv())
        nears[lag - 1].wait_recv()
        aways[lag].wait_recv()

    def leave(step):
        cols = pl.ds(pl.multiple_of(step * WIDE, WIDE), WIDE)
        return pltpu.make_async_copy(out.at[:, cols], out_hbm.at[:, cols], out_sem.at[step])

    for lag in spans:
        if lag == 0:
            aways[0].wait_recv()
        else:
            pl.when(seq >= lag)(functools.partial(arrived, lag))
        scaled(lag)

    def convolve(step, carry):
        cols = pl.ds(pl.multiple_of(step * WIDE, WIDE), WIDE)
        acc_re = acc_im = None
        for lag in spans:
            block = xv[:, cols] if lag == 0 else halo[lag - 1, :, cols]
            here = jnp.dot(
                fs[lag], jnp.concatenate([block, block], 0), preferred_element_type=jnp.float32
            )
            re, im = here[:B], here[B:]
            sre, sim = spec[lag, :B, cols], spec[lag, B:, cols]
            new_re, new_im = re * sre - im * sim, re * sim + im * sre
            acc_re = new_re if lag == 0 else acc_re + new_re
            acc_im = new_im if lag == 0 else acc_im + new_im
        hi, lo = split(jnp.concatenate([acc_re, acc_im], 0))
        ihi, ilo = icat[:, : 2 * B], icat[:, 2 * B :]
        result = (
            jnp.dot(ihi, hi, preferred_element_type=jnp.float32)
            + jnp.dot(ihi, lo, preferred_element_type=jnp.float32)
            + jnp.dot(ilo, hi, preferred_element_type=jnp.float32)
        )
        out[:, cols] = (gate[:, cols].astype(jnp.float32) * result).astype(jnp.bfloat16)
        leave(step).start()
        return carry

    wides = xv.shape[1] // WIDE
    lax.fori_loop(0, wides, convolve, 0)

    for step in range(wides):
        leave(step).wait()
    each(xs, lambda copy: copy.wait_send())
    for k in spans:
        pl.when(has(k))(lambda copy=aways[k]: copy.wait_send())
    for k in lags:
        pl.when(has(k))(lambda copy=nears[k - 1]: copy.wait_send())

    def sent(copies):
        each(copies, lambda copy: copy.wait_send())

    pl.when(has(2))(lambda: sent(own))
    pl.when(jnp.logical_and(has(2), has(-2)))(lambda: sent(onward))
    pl.when(even)(lambda: sent(even_first))
    pl.when(jnp.logical_and(even, has(-2)))(lambda: sent(even_second))
    pl.when(jnp.logical_and(odd, has(-2)))(lambda: sent(odd_first))
    pl.when(jnp.logical_and(odd, has(-4)))(lambda: sent(odd_second))


def on_device(inputs, gating, long_filter, skip_scale):
    rows, channels = inputs.shape
    bf16, f32 = jnp.bfloat16, jnp.float32
    ftab, fcat, icat = tables()
    dma = pltpu.SemaphoreType.DMA
    return pl.pallas_call(
        kernel,
        out_shape=jax.ShapeDtypeStruct((rows, channels), bf16),
        in_specs=[pl.BlockSpec(memory_space=pltpu.HBM)] * 7,
        out_specs=pl.BlockSpec(memory_space=pl.ANY),
        scratch_shapes=[
            pltpu.VMEM((rows, channels), bf16),
            pltpu.VMEM((rows, channels), bf16),
            pltpu.VMEM(long_filter.shape, bf16),
            pltpu.VMEM((1, channels), f32),
            pltpu.VMEM(ftab.shape, f32),
            pltpu.VMEM(fcat.shape, bf16),
            pltpu.VMEM(icat.shape, bf16),
            pltpu.VMEM((LAGS, rows, channels), bf16),
            pltpu.VMEM((LAGS + 1, 2 * B, channels), f32),
            pltpu.VMEM((LAGS + 1, 2 * B, 2 * B), bf16),
            pltpu.VMEM((rows, channels), bf16),
            pltpu.VMEM((1, B), f32),
            pltpu.VMEM((3, 1, B), f32),
            pltpu.VMEM((1, B), f32),
            pltpu.VMEM((LAGS, 1, B), f32),
            pltpu.VMEM((LAGS + 1, 1, B), f32),
            dma((7,)),
            dma((CHUNKS,)),
            dma((CHUNKS,)),
            dma((2, CHUNKS)),
            dma((LAGS, CHUNKS)),
            dma((3,)),
            dma((3,)),
            dma((LAGS,)),
            dma((LAGS,)),
            dma((LAGS + 1,)),
            dma((LAGS + 1,)),
            pltpu.SemaphoreType.REGULAR,
            pltpu.SemaphoreType.REGULAR((LAGS,)),
            dma((channels // WIDE,)),
        ],
        compiler_params=pltpu.CompilerParams(
            collective_id=0, has_side_effects=True, vmem_limit_bytes=60 * 1024 * 1024
        ),
    )(inputs, gating, long_filter, skip_scale[None, :], ftab, fcat, icat)


def solution(mesh):
    in_specs = (P("seq", "chan"), P("seq", "chan"), P(None, "chan"), P("chan"))
    return jax.shard_map(
        on_device, mesh=mesh, in_specs=in_specs, out_specs=P("seq", "chan"), check_vma=False
    )
```

```python
import functools

import jax
import jax.numpy as jnp
import numpy as np
from jax import lax
from jax.experimental import pallas as pl
from jax.experimental.pallas import tpu as pltpu
from jax.sharding import PartitionSpec as P

D = 8192
MESH = pl.DeviceIdType.MESH
B = 128
LAGS = 4
CW = 256
WIDE = 512
CHUNKS = 4
ROWS = B // CHUNKS


def split(value):
    hi = value.astype(jnp.bfloat16)
    return hi, (value - hi.astype(jnp.float32)).astype(jnp.bfloat16)


def tables():
    bins = np.concatenate([np.arange(0, B, 2), np.arange(1, B, 2)])
    angle = np.pi * np.outer(2 * bins + 1, np.arange(B)) / (2 * B)
    forward = np.concatenate([np.cos(angle), -np.sin(angle)], 0)
    inverse = forward.T / B

    def halves(table):
        table = table.astype(np.float32)
        hi = table.astype(jnp.bfloat16)
        lo = (table - hi.astype(np.float32)).astype(jnp.bfloat16)
        return np.concatenate([hi, lo], 1)

    return forward.astype(np.float32), halves(forward), halves(inverse)


def kernel(
    x_hbm,
    gate_hbm,
    taps_hbm,
    skip_hbm,
    ftab_hbm,
    fcat_hbm,
    icat_hbm,
    out_hbm,
    xv,
    gate,
    taps,
    skip,
    ftab,
    fcat,
    icat,
    halo,
    spec,
    fs,
    out,
    part,
    xpart,
    xsum,
    near,
    away,
    handed_sum,
    load_sem,
    own_send,
    fwd_send,
    mate_send,
    halo_recv,
    x_send,
    x_recv,
    near_send,
    near_recv,
    away_send,
    away_recv,
    ready,
    go,
    out_sem,
    hub_send,
    hub_recv,
):
    seq, chan = lax.axis_index("seq"), lax.axis_index("chan")
    count = lax.axis_size("seq")
    half, col = lax.div(chan, 4), lax.rem(chan, 4)
    upper = half == 1
    odd = lax.rem(seq, 2) == 1
    even = jnp.logical_not(odd)
    lags = range(1, LAGS + 1)
    spans = range(LAGS + 1)

    def ahead(k):
        return (seq + k, chan)

    def across(k):
        return (seq + k, (1 - half) * 4 + col)

    def beside(shift):
        return (seq, half * 4 + lax.rem(col + shift, 4))

    row, side = lax.div(seq, 8), lax.rem(lax.div(seq, 2), 4) == 3
    hub = jnp.logical_and(side, lax.rem(row, 2) == 1)
    spoke = jnp.logical_and(side, lax.rem(row, 2) == 0)
    lower = jnp.logical_not(upper)

    def both(*conditions):
        return functools.reduce(jnp.logical_and, conditions)

    def has(k):
        return jnp.logical_and(seq + k >= 0, seq + k < count)

    def signal(sem, device):
        pl.semaphore_signal(sem, inc=1, device_id=device, device_id_type=MESH)

    loads = [
        pltpu.make_async_copy(src, dst, load_sem.at[n])
        for n, (src, dst) in enumerate(
            [
                (x_hbm, xv),
                (fcat_hbm, fcat),
                (taps_hbm, taps),
                (skip_hbm, skip),
                (ftab_hbm, ftab),
                (icat_hbm, icat),
                (gate_hbm, gate),
            ]
        )
    ]

    loads[0].start()
    barrier = pltpu.get_barrier_semaphore()
    @pl.when(lower)
    def _():
        for k in range(-LAGS, LAGS + 1):
            pl.when(has(k))(functools.partial(signal, barrier, across(k)))
        pl.when(hub)(functools.partial(signal, barrier, across(-8)))

        @pl.when(spoke)
        def _():
            signal(barrier, ahead(8))
            pl.when(odd)(functools.partial(signal, barrier, ahead(7)))

    for shift in (1, 2, 3):
        signal(barrier, beside(shift))
    for k in lags:
        pl.when(has(k))(functools.partial(signal, barrier, ahead(k)))

    for load in loads[1:]:
        load.start()

    loads[0].wait()
    gram = lax.dot_general(
        xv[...], xv[...], (((1,), (1,)), ((), ())), preferred_element_type=jnp.float32
    )
    diagonal = lax.broadcasted_iota(jnp.int32, (B, B), 0) == lax.broadcasted_iota(
        jnp.int32, (B, B), 1
    )
    part[...] = jnp.sum(jnp.where(diagonal, gram, 0.0), axis=0, keepdims=True)

    before, after = jnp.minimum(seq, LAGS), jnp.minimum(count - 1 - seq, LAGS)
    far = half * (before + after + 1 + spoke.astype(jnp.int32))
    extra = (1 - half) * hub.astype(jnp.int32) * (2 - lax.rem(seq, 2))
    pl.semaphore_wait(barrier, 3 + before + far + extra)

    @pl.when(upper)
    def _():
        for k in spans:
            pl.when(has(-k))(functools.partial(signal, ready, across(-k)))

    def remote(src, dst, send, recv, device):
        return pltpu.make_async_remote_copy(
            src_ref=src,
            dst_ref=dst,
            send_sem=send,
            recv_sem=recv,
            device_id=device,
            device_id_type=MESH,
        )

    def piece(n):
        return pl.ds(n * ROWS, ROWS)

    def to_next(src, slot, n, send):
        return remote(
            src.at[piece(n)], halo.at[slot, piece(n)], send.at[n], halo_recv.at[slot, n], ahead(2)
        )

    def to_mate(src, slot, n):
        return remote(
            src.at[piece(n)],
            halo.at[slot, piece(n)],
            mate_send.at[slot // 2, n],
            halo_recv.at[slot, n],
            ahead(1 - 2 * lax.rem(seq, 2)),
        )

    pieces = range(CHUNKS)
    own = [to_next(x_hbm, 1, n, own_send) for n in pieces]
    onward = [to_next(halo.at[1], 3, n, fwd_send) for n in pieces]
    even_first = [to_mate(x_hbm, 0, n) for n in pieces]
    even_second = [to_mate(halo.at[1], 2, n) for n in pieces]
    odd_first = [to_mate(halo.at[1], 0, n) for n in pieces]
    odd_second = [to_mate(halo.at[3], 2, n) for n in pieces]

    def each(copies, act):
        for copy in copies:
            act(copy)

    xs = [
        remote(part, xpart.at[d - 1], x_send.at[d - 1], x_recv.at[d - 1], beside(d))
        for d in (1, 2, 3)
    ]
    each(xs, lambda copy: copy.start())

    for k in (2, 1, 3, 4):
        pl.when(has(-k))(functools.partial(signal, go.at[k - 1], ahead(-k)))

    for k in lags:

        @pl.when(seq < k)
        def _():
            halo[k - 1] = jnp.zeros(halo.shape[1:], halo.dtype)

    each(loads[1:4], lambda copy: copy.wait())

    def filter_spectra(step, carry):
        cols = pl.ds(pl.multiple_of(step * CW, CW), CW)
        last_re = last_im = None
        for lag in spans:
            if lag < LAGS:
                block = taps[lag * B : (lag + 1) * B, cols]
                here = jnp.dot(
                    fcat[...],
                    jnp.concatenate([block, block], 0),
                    preferred_element_type=jnp.float32,
                )
                re, im = here[:B], here[B:]
                full_re, full_im = (re + skip[:, cols] if lag == 0 else re), im
            else:
                tap = taps[LAGS * B : LAGS * B + 1, cols].astype(jnp.float32)
                full_re, full_im = jnp.broadcast_to(tap, (B, CW)), jnp.zeros((B, CW), jnp.float32)
            if last_re is not None:
                h = B // 2
                turned_re = jnp.concatenate([-last_im[:h], last_im[h:]], 0)
                turned_im = jnp.concatenate([last_re[:h], -last_re[h:]], 0)
                full_re, full_im = full_re + turned_re, full_im + turned_im
            spec[lag, :B, cols] = full_re
            spec[lag, B:, cols] = full_im
            if lag < LAGS:
                last_re, last_im = re, im
        return carry

    steps = xv.shape[1] // CW
    lax.fori_loop(0, steps, filter_spectra, 0)

    @pl.when(has(2))
    def _():
        pl.semaphore_wait(go.at[1], 1)
        each(own, lambda copy: copy.start())

    @pl.when(has(1))
    def _():
        pl.semaphore_wait(go.at[0], 1)

        @pl.when(even)
        def _():
            each(even_first, lambda copy: copy.start())

    each(xs, lambda copy: copy.wait_recv())
    xsum[...] = part[...] + xpart[0] + xpart[1] + xpart[2]
    nears = [
        remote(xsum, near.at[k - 1], near_send.at[k - 1], near_recv.at[k - 1], ahead(k))
        for k in lags
    ]
    aways = [
        remote(xsum, away.at[k], away_send.at[k], away_recv.at[k], across(k)) for k in spans
    ]

    def direct(k):
        if k > 1:
            return has(k)
        handed = both(upper, spoke) if k == 0 else both(upper, spoke, even)
        return both(has(k), jnp.logical_not(handed))

    to_hub = remote(xsum, handed_sum, hub_send.at[0], hub_recv, across(8))
    from_hub = [
        remote(handed_sum, away.at[k], hub_send.at[k + 1], away_recv.at[k], ahead(k - 8))
        for k in (0, 1)
    ]

    def send_away():
        pl.when(both(upper, spoke))(lambda: to_hub.start())
        for k in spans:
            pl.when(direct(k))(lambda copy=aways[k]: copy.start())

    pl.when(upper)(send_away)
    for k in lags:

        @pl.when(has(k))
        def _():
            if k > 2:
                pl.semaphore_wait(go.at[k - 1], 1)
            nears[k - 1].start()

    @pl.when(has(-2))
    def _():
        for n in pieces:
            own[n].wait_recv()
            pl.when(has(2))(lambda n=n: onward[n].start())
            pl.when(odd)(lambda n=n: odd_first[n].start())
            pl.when(even)(lambda n=n: even_second[n].start())

    @pl.when(jnp.logical_not(upper))
    def _():
        pl.semaphore_wait(ready, after + 1)
        send_away()

        @pl.when(hub)
        def _():
            to_hub.wait_recv()
            from_hub[0].start()
            pl.when(even)(lambda: from_hub[1].start())

    @pl.when(has(-4))
    def _():
        for n in pieces:
            onward[n].wait_recv()
            pl.when(odd)(lambda n=n: odd_second[n].start())

    each(loads[4:], lambda copy: copy.wait())

    def scaled(lag):
        if lag == 0:
            sums = xsum[...] + away[0]
        else:
            sums = near[lag - 1] + away[lag]
        scale = lax.rsqrt(sums * (1.0 / D) + 1e-06)
        if lag:
            scale = jnp.where(seq >= lag, scale, 0.0)
        hi, lo = split(ftab[...] * scale)
        fs[lag, :, :B] = hi
        fs[lag, :, B:] = lo

    def arrived(lag):
        if lag in (1, 3):
            each(odd_first if lag == 1 else odd_second, lambda copy: copy.wait_recv())
        nears[lag - 1].wait_recv()
        aways[lag].wait_recv()

    def leave(step):
        cols = pl.ds(pl.multiple_of(step * WIDE, WIDE), WIDE)
        return pltpu.make_async_copy(out.at[:, cols], out_hbm.at[:, cols], out_sem.at[step])

    for lag in spans:
        if lag == 0:
            aways[0].wait_recv()
        else:
            pl.when(seq >= lag)(functools.partial(arrived, lag))
        scaled(lag)

    def convolve(step, carry):
        cols = pl.ds(pl.multiple_of(step * WIDE, WIDE), WIDE)
        acc_re = acc_im = None
        for lag in spans:
            block = xv[:, cols] if lag == 0 else halo[lag - 1, :, cols]
            here = jnp.dot(
                fs[lag], jnp.concatenate([block, block], 0), preferred_element_type=jnp.float32
            )
            re, im = here[:B], here[B:]
            sre, sim = spec[lag, :B, cols], spec[lag, B:, cols]
            new_re, new_im = re * sre - im * sim, re * sim + im * sre
            acc_re = new_re if lag == 0 else acc_re + new_re
            acc_im = new_im if lag == 0 else acc_im + new_im
        hi, lo = split(jnp.concatenate([acc_re, acc_im], 0))
        ihi, ilo = icat[:, : 2 * B], icat[:, 2 * B :]
        result = (
            jnp.dot(ihi, hi, preferred_element_type=jnp.float32)
            + jnp.dot(ihi, lo, preferred_element_type=jnp.float32)
            + jnp.dot(ilo, hi, preferred_element_type=jnp.float32)
        )
        out[:, cols] = (gate[:, cols].astype(jnp.float32) * result).astype(jnp.bfloat16)
        leave(step).start()
        return carry

    wides = xv.shape[1] // WIDE
    lax.fori_loop(0, wides, convolve, 0)

    for step in range(wides):
        leave(step).wait()
    each(xs, lambda copy: copy.wait_send())
    for k in spans:
        pl.when(direct(k))(lambda copy=aways[k]: copy.wait_send())
    pl.when(both(upper, spoke))(lambda: to_hub.wait_send())
    pl.when(both(lower, hub))(lambda: from_hub[0].wait_send())
    pl.when(both(lower, hub, even))(lambda: from_hub[1].wait_send())
    for k in lags:
        pl.when(has(k))(lambda copy=nears[k - 1]: copy.wait_send())

    def sent(copies):
        each(copies, lambda copy: copy.wait_send())

    pl.when(has(2))(lambda: sent(own))
    pl.when(jnp.logical_and(has(2), has(-2)))(lambda: sent(onward))
    pl.when(even)(lambda: sent(even_first))
    pl.when(jnp.logical_and(even, has(-2)))(lambda: sent(even_second))
    pl.when(jnp.logical_and(odd, has(-2)))(lambda: sent(odd_first))
    pl.when(jnp.logical_and(odd, has(-4)))(lambda: sent(odd_second))


def on_device(inputs, gating, long_filter, skip_scale):
    rows, channels = inputs.shape
    bf16, f32 = jnp.bfloat16, jnp.float32
    ftab, fcat, icat = tables()
    dma = pltpu.SemaphoreType.DMA
    return pl.pallas_call(
        kernel,
        out_shape=jax.ShapeDtypeStruct((rows, channels), bf16),
        in_specs=[pl.BlockSpec(memory_space=pltpu.HBM)] * 7,
        out_specs=pl.BlockSpec(memory_space=pl.ANY),
        scratch_shapes=[
            pltpu.VMEM((rows, channels), bf16),
            pltpu.VMEM((rows, channels), bf16),
            pltpu.VMEM(long_filter.shape, bf16),
            pltpu.VMEM((1, channels), f32),
            pltpu.VMEM(ftab.shape, f32),
            pltpu.VMEM(fcat.shape, bf16),
            pltpu.VMEM(icat.shape, bf16),
            pltpu.VMEM((LAGS, rows, channels), bf16),
            pltpu.VMEM((LAGS + 1, 2 * B, channels), f32),
            pltpu.VMEM((LAGS + 1, 2 * B, 2 * B), bf16),
            pltpu.VMEM((rows, channels), bf16),
            pltpu.VMEM((1, B), f32),
            pltpu.VMEM((3, 1, B), f32),
            pltpu.VMEM((1, B), f32),
            pltpu.VMEM((LAGS, 1, B), f32),
            pltpu.VMEM((LAGS + 1, 1, B), f32),
            pltpu.VMEM((1, B), f32),
            dma((7,)),
            dma((CHUNKS,)),
            dma((CHUNKS,)),
            dma((2, CHUNKS)),
            dma((LAGS, CHUNKS)),
            dma((3,)),
            dma((3,)),
            dma((LAGS,)),
            dma((LAGS,)),
            dma((LAGS + 1,)),
            dma((LAGS + 1,)),
            pltpu.SemaphoreType.REGULAR,
            pltpu.SemaphoreType.REGULAR((LAGS,)),
            dma((channels // WIDE,)),
            dma((3,)),
            dma,
        ],
        compiler_params=pltpu.CompilerParams(
            collective_id=0, has_side_effects=True, vmem_limit_bytes=60 * 1024 * 1024
        ),
    )(inputs, gating, long_filter, skip_scale[None, :], ftab, fcat, icat)


def solution(mesh):
    in_specs = (P("seq", "chan"), P("seq", "chan"), P(None, "chan"), P("chan"))
    return jax.shard_map(
        on_device, mesh=mesh, in_specs=in_specs, out_specs=P("seq", "chan"), check_vma=False
    )
```

```python
import functools

import jax
import jax.numpy as jnp
import numpy as np
from jax import lax
from jax.experimental import pallas as pl
from jax.experimental.pallas import tpu as pltpu
from jax.sharding import PartitionSpec as P

D = 8192
MESH = pl.DeviceIdType.MESH
B = 128
LAGS = 4
CW = 256
WIDE = 512
CHUNKS = 2
ROWS = B // CHUNKS


def split(value):
    hi = value.astype(jnp.bfloat16)
    return hi, (value - hi.astype(jnp.float32)).astype(jnp.bfloat16)


def tables():
    bins = np.concatenate([np.arange(0, B, 2), np.arange(1, B, 2)])
    angle = np.pi * np.outer(2 * bins + 1, np.arange(B)) / (2 * B)
    forward = np.concatenate([np.cos(angle), -np.sin(angle)], 0)
    inverse = forward.T / B

    def halves(table):
        table = table.astype(np.float32)
        hi = table.astype(jnp.bfloat16)
        return [hi, (table - hi.astype(np.float32)).astype(jnp.bfloat16)]

    return np.concatenate([np.concatenate(halves(forward), 1)] + halves(inverse), 0)


def kernel(
    x_hbm,
    gate_hbm,
    taps_hbm,
    skip_hbm,
    tab_hbm,
    out_hbm,
    xv,
    gate,
    taps,
    skip,
    tab,
    halo,
    spec,
    fs,
    out,
    part,
    xpart,
    xsum,
    near,
    away,
    handed_sum,
    load_sem,
    next_send,
    mate_send,
    next_recv,
    mate_recv,
    x_sem,
    near_sem,
    away_sem,
    hub_sem,
    greet,
    out_sem,
):
    seq, chan = lax.axis_index("seq"), lax.axis_index("chan")
    count = lax.axis_size("seq")
    half, col = lax.div(chan, 4), lax.rem(chan, 4)
    upper = half == 1
    odd = lax.rem(seq, 2) == 1
    even = jnp.logical_not(odd)
    lags = range(1, LAGS + 1)
    spans = range(LAGS + 1)

    def ahead(k):
        return (seq + k, chan)

    def across(k):
        return (seq + k, (1 - half) * 4 + col)

    def beside(shift):
        return (seq, half * 4 + lax.rem(col + shift, 4))

    row, side = lax.div(seq, 8), lax.rem(lax.div(seq, 2), 4) == 3
    hub = jnp.logical_and(side, lax.rem(row, 2) == 1)
    spoke = jnp.logical_and(side, lax.rem(row, 2) == 0)
    lower = jnp.logical_not(upper)

    def both(*conditions):
        return functools.reduce(jnp.logical_and, conditions)

    def has(k):
        return jnp.logical_and(seq + k >= 0, seq + k < count)

    def signal(sem, device):
        pl.semaphore_signal(sem, inc=1, device_id=device, device_id_type=MESH)

    loads = [
        pltpu.make_async_copy(src, dst, load_sem.at[n])
        for n, (src, dst) in enumerate(
            [
                (x_hbm, xv),
                (tab_hbm, tab),
                (taps_hbm, taps),
                (skip_hbm, skip),
                (gate_hbm, gate),
            ]
        )
    ]

    loads[0].start()
    barrier = pltpu.get_barrier_semaphore()
    @pl.when(lower)
    def _():
        for k in range(-LAGS, LAGS + 1):
            pl.when(has(k))(functools.partial(signal, barrier, across(k)))
        pl.when(hub)(functools.partial(signal, barrier, across(-8)))

        @pl.when(spoke)
        def _():
            signal(barrier, ahead(8))
            pl.when(odd)(functools.partial(signal, barrier, ahead(7)))

    for shift in (1, 2, 3):
        signal(barrier, beside(shift))
    for k in lags:
        pl.when(has(k))(functools.partial(signal, barrier, ahead(k)))

    for load in loads[1:]:
        load.start()

    loads[0].wait()
    gram = lax.dot_general(
        xv[...], xv[...], (((1,), (1,)), ((), ())), preferred_element_type=jnp.float32
    )
    diagonal = lax.broadcasted_iota(jnp.int32, (B, B), 0) == lax.broadcasted_iota(
        jnp.int32, (B, B), 1
    )
    part[...] = jnp.sum(jnp.where(diagonal, gram, 0.0), axis=0, keepdims=True)

    before, after = jnp.minimum(seq, LAGS), jnp.minimum(count - 1 - seq, LAGS)
    far = half * (before + after + 1 + spoke.astype(jnp.int32))
    extra = (1 - half) * hub.astype(jnp.int32) * (2 - lax.rem(seq, 2))
    pl.semaphore_wait(barrier, 3 + before + far + extra)

    @pl.when(upper)
    def _():
        for k in spans:
            pl.when(has(-k))(functools.partial(signal, greet.at[2], across(-k)))

    def remote(src, dst, send, recv, device):
        return pltpu.make_async_remote_copy(
            src_ref=src,
            dst_ref=dst,
            send_sem=send,
            recv_sem=recv,
            device_id=device,
            device_id_type=MESH,
        )

    def piece(n):
        return pl.ds(n * ROWS, ROWS)

    def to_next(src, slot, n, rows):
        return remote(
            src.at[rows],
            halo.at[slot, rows],
            next_send.at[slot // 2],
            next_recv.at[slot // 2, n],
            ahead(2),
        )

    def to_mate(src, slot, rows):
        return remote(
            src.at[rows],
            halo.at[slot, rows],
            mate_send.at[slot // 2],
            mate_recv.at[slot // 2],
            ahead(1 - 2 * lax.rem(seq, 2)),
        )

    pieces = range(CHUNKS)
    whole = pl.ds(0, B)
    own = [to_next(x_hbm, 1, n, piece(n)) for n in pieces]
    onward = [to_next(halo.at[1], 3, n, piece(n)) for n in pieces]
    even_first = to_mate(x_hbm, 0, whole)
    even_second = [to_mate(halo.at[1], 2, piece(n)) for n in pieces]
    odd_first = [to_mate(halo.at[1], 0, piece(n)) for n in pieces]
    odd_second = [to_mate(halo.at[3], 2, piece(n)) for n in pieces]
    all_next = [to_next(halo.at[slot], slot, 0, whole) for slot in (1, 3)]
    all_mate = [to_mate(halo.at[slot], slot, whole) for slot in (0, 2)]

    def gather(ref, sems, amount, most):
        def on(act):
            for n in range(1, most + 1):
                rows = ref.at[pl.ds(0, n)]
                copy = remote(rows, rows, sems.at[0], sems.at[1], beside(1))
                pl.when(amount == n)(functools.partial(act, copy))

        return on

    def each(copies, act):
        for copy in copies:
            act(copy)

    xs = [
        remote(part, xpart.at[d - 1], x_sem.at[0], x_sem.at[1], beside(d))
        for d in (1, 2, 3)
    ]
    each(xs, lambda copy: copy.start())

    for k in (2, 1, 3, 4):
        pl.when(has(-k))(functools.partial(signal, greet.at[(k - 1) // 2], ahead(-k)))

    for k in lags:

        @pl.when(seq < k)
        def _():
            halo[k - 1] = jnp.zeros(halo.shape[1:], halo.dtype)

    every_x = remote(xpart, xpart, x_sem.at[0], x_sem.at[1], beside(1))

    each(loads[1:4], lambda copy: copy.wait())

    def filter_spectra(step, carry):
        cols = pl.ds(pl.multiple_of(step * CW, CW), CW)
        last_re = last_im = None
        for lag in spans:
            if lag < LAGS:
                block = taps[lag * B : (lag + 1) * B, cols]
                here = jnp.dot(
                    tab[: 2 * B],
                    jnp.concatenate([block, block], 0),
                    preferred_element_type=jnp.float32,
                )
                re, im = here[:B], here[B:]
                full_re, full_im = (re + skip[:, cols] if lag == 0 else re), im
            else:
                tap = taps[LAGS * B : LAGS * B + 1, cols].astype(jnp.float32)
                full_re, full_im = jnp.broadcast_to(tap, (B, CW)), jnp.zeros((B, CW), jnp.float32)
            if last_re is not None:
                h = B // 2
                turned_re = jnp.concatenate([-last_im[:h], last_im[h:]], 0)
                turned_im = jnp.concatenate([last_re[:h], -last_re[h:]], 0)
                full_re, full_im = full_re + turned_re, full_im + turned_im
            spec[lag, :B, cols] = full_re
            spec[lag, B:, cols] = full_im
            if lag < LAGS:
                last_re, last_im = re, im
        return carry

    steps = xv.shape[1] // CW
    lax.fori_loop(0, steps, filter_spectra, 0)

    pl.when(has(1))(lambda: pl.semaphore_wait(greet.at[0], jnp.minimum(after, 2)))
    pl.when(has(2))(lambda: each(own, lambda copy: copy.start()))
    pl.when(even)(lambda: even_first.start())
    every_x.wait_recv()
    xsum[...] = part[...] + xpart[0] + xpart[1] + xpart[2]
    nears = [
        remote(xsum, near.at[k - 1], near_sem.at[0], near_sem.at[1], ahead(k))
        for k in lags
    ]
    aways = [
        remote(xsum, away.at[k], away_sem.at[0], away_sem.at[1], across(k)) for k in spans
    ]

    def direct(k):
        if k > 1:
            return has(k)
        handed = both(upper, spoke) if k == 0 else both(upper, spoke, even)
        return both(has(k), jnp.logical_not(handed))

    to_hub = remote(xsum, handed_sum.at[0], away_sem.at[0], hub_sem.at[1], across(8))
    from_hub = [
        remote(handed_sum.at[0], away.at[k], hub_sem.at[0], away_sem.at[1], ahead(k - 8))
        for k in (0, 1)
    ]

    def send_away():
        pl.when(both(upper, spoke))(lambda: to_hub.start())
        for k in spans:
            pl.when(direct(k))(lambda copy=aways[k]: copy.start())

    pl.when(upper)(send_away)
    pl.when(has(3))(lambda: pl.semaphore_wait(greet.at[1], after - 2))
    for k in lags:
        pl.when(has(k))(lambda copy=nears[k - 1]: copy.start())

    @pl.when(has(-2))
    def _():
        for n in pieces:
            own[n].wait_recv()
            pl.when(has(2))(lambda n=n: onward[n].start())
            pl.when(odd)(lambda n=n: odd_first[n].start())
            pl.when(even)(lambda n=n: even_second[n].start())

    @pl.when(jnp.logical_not(upper))
    def _():
        pl.semaphore_wait(greet.at[2], after + 1)
        send_away()

        @pl.when(hub)
        def _():
            to_hub.wait_recv()
            from_hub[0].start()
            pl.when(even)(lambda: from_hub[1].start())

    @pl.when(has(-4))
    def _():
        for n in pieces:
            onward[n].wait_recv()
            pl.when(odd)(lambda n=n: odd_second[n].start())

    each(loads[4:], lambda copy: copy.wait())

    def scaled(lag):
        if lag == 0:
            sums = xsum[...] + away[0]
        else:
            sums = near[lag - 1] + away[lag]
        scale = lax.rsqrt(sums * (1.0 / D) + 1e-06)
        if lag:
            scale = jnp.where(seq >= lag, scale, 0.0)
        hi, lo = split((tab[: 2 * B, :B].astype(jnp.float32) + tab[: 2 * B, B:].astype(jnp.float32)) * scale)
        fs[lag, :, :B] = hi
        fs[lag, :, B:] = lo

    def leave(step):
        cols = pl.ds(pl.multiple_of(step * WIDE, WIDE), WIDE)
        return pltpu.make_async_copy(out.at[:, cols], out_hbm.at[:, cols], out_sem)

    def sent(*copies):
        each(copies, lambda copy: copy.wait_send())

    every_x.wait_send()
    gather(near, near_sem, after, LAGS)(lambda copy: copy.wait_send())
    pl.when(has(2))(lambda: sent(all_next[0]))
    pl.when(both(has(2), has(-2)))(lambda: sent(all_next[1]))
    pl.when(jnp.logical_or(even, has(-2)))(lambda: sent(all_mate[0]))
    pl.when(jnp.logical_or(both(even, has(-2)), has(-4)))(lambda: sent(all_mate[1]))
    pl.when(has(-1))(lambda: all_mate[0].wait_recv())
    pl.when(has(-3))(lambda: all_mate[1].wait_recv())
    gather(near, near_sem, before, LAGS)(lambda copy: copy.wait_recv())
    gather(away, away_sem, before + 1, LAGS + 1)(lambda copy: copy.wait_recv())
    for lag in spans:
        scaled(lag)

    def convolve(step, carry):
        cols = pl.ds(pl.multiple_of(step * WIDE, WIDE), WIDE)
        acc_re = acc_im = None
        for lag in spans:
            block = xv[:, cols] if lag == 0 else halo[lag - 1, :, cols]
            here = jnp.dot(
                fs[lag], jnp.concatenate([block, block], 0), preferred_element_type=jnp.float32
            )
            re, im = here[:B], here[B:]
            sre, sim = spec[lag, :B, cols], spec[lag, B:, cols]
            new_re, new_im = re * sre - im * sim, re * sim + im * sre
            acc_re = new_re if lag == 0 else acc_re + new_re
            acc_im = new_im if lag == 0 else acc_im + new_im
        hi, lo = split(jnp.concatenate([acc_re, acc_im], 0))
        ihi, ilo = tab[2 * B : 3 * B], tab[3 * B :]
        result = (
            jnp.dot(ihi, hi, preferred_element_type=jnp.float32)
            + jnp.dot(ihi, lo, preferred_element_type=jnp.float32)
            + jnp.dot(ilo, hi, preferred_element_type=jnp.float32)
        )
        out[:, cols] = (gate[:, cols].astype(jnp.float32) * result).astype(jnp.bfloat16)
        leave(step).start()
        return carry

    wides = xv.shape[1] // WIDE
    lax.fori_loop(0, wides, convolve, 0)

    left = after + 1 - both(upper, spoke, even).astype(jnp.int32)
    gather(away, away_sem, left, LAGS + 1)(lambda copy: copy.wait_send())
    handed_on = both(lower, hub).astype(jnp.int32) * (2 - lax.rem(seq, 2))
    gather(handed_sum, hub_sem, handed_on, 2)(lambda copy: copy.wait_send())
    pltpu.make_async_copy(out, out_hbm, out_sem).wait()


def on_device(inputs, gating, long_filter, skip_scale):
    rows, channels = inputs.shape
    bf16, f32 = jnp.bfloat16, jnp.float32
    tab = tables()
    dma = pltpu.SemaphoreType.DMA
    return pl.pallas_call(
        kernel,
        out_shape=jax.ShapeDtypeStruct((rows, channels), bf16),
        in_specs=[pl.BlockSpec(memory_space=pltpu.HBM)] * 5,
        out_specs=pl.BlockSpec(memory_space=pl.ANY),
        scratch_shapes=[
            pltpu.VMEM((rows, channels), bf16),
            pltpu.VMEM((rows, channels), bf16),
            pltpu.VMEM(long_filter.shape, bf16),
            pltpu.VMEM((1, channels), f32),
            pltpu.VMEM(tab.shape, bf16),
            pltpu.VMEM((LAGS, rows, channels), bf16),
            pltpu.VMEM((LAGS + 1, 2 * B, channels), f32),
            pltpu.VMEM((LAGS + 1, 2 * B, 2 * B), bf16),
            pltpu.VMEM((rows, channels), bf16),
            pltpu.VMEM((1, B), f32),
            pltpu.VMEM((3, 1, B), f32),
            pltpu.VMEM((1, B), f32),
            pltpu.VMEM((LAGS, 1, B), f32),
            pltpu.VMEM((LAGS + 1, 1, B), f32),
            pltpu.VMEM((2, 1, B), f32),
            dma((5,)),
            dma((2,)),
            dma((2,)),
            dma((2, CHUNKS)),
            dma((2,)),
            dma((2,)),
            dma((2,)),
            dma((2,)),
            dma((2,)),
            pltpu.SemaphoreType.REGULAR((3,)),
            dma,
        ],
        compiler_params=pltpu.CompilerParams(
            collective_id=0, has_side_effects=True, vmem_limit_bytes=60 * 1024 * 1024
        ),
    )(inputs, gating, long_filter, skip_scale[None, :], tab)


def solution(mesh):
    in_specs = (P("seq", "chan"), P("seq", "chan"), P(None, "chan"), P("chan"))
    return jax.shard_map(
        on_device, mesh=mesh, in_specs=in_specs, out_specs=P("seq", "chan"), check_vma=False
    )
```

```python
import functools

import jax
import jax.numpy as jnp
import numpy as np
from jax import lax
from jax.experimental import pallas as pl
from jax.experimental.pallas import tpu as pltpu
from jax.sharding import PartitionSpec as P

D = 8192
MESH = pl.DeviceIdType.MESH
B = 128
LAGS = 4
CW = 256
WIDE = 512
CHUNKS = 4
ROWS = B // CHUNKS


def split(value):
    hi = value.astype(jnp.bfloat16)
    return hi, (value - hi.astype(jnp.float32)).astype(jnp.bfloat16)


def tables():
    bins = np.concatenate([np.arange(0, B, 2), np.arange(1, B, 2)])
    angle = np.pi * np.outer(2 * bins + 1, np.arange(B)) / (2 * B)
    forward = np.concatenate([np.cos(angle), -np.sin(angle)], 0)
    inverse = forward.T / B

    def halves(table):
        table = table.astype(np.float32)
        hi = table.astype(jnp.bfloat16)
        return [hi, (table - hi.astype(np.float32)).astype(jnp.bfloat16)]

    return np.concatenate([np.concatenate(halves(forward), 1)] + halves(inverse), 0)


def kernel(
    x_hbm,
    gate_hbm,
    taps_hbm,
    skip_hbm,
    tab_hbm,
    out_hbm,
    xv,
    gate,
    taps,
    skip,
    tab,
    halo,
    spec,
    fs,
    out,
    part,
    xpart,
    xsum,
    near,
    away,
    handed_sum,
    load_sem,
    next_send,
    mate_send,
    next_recv,
    mate_recv,
    x_sem,
    near_sem,
    away_sem,
    hub_sem,
    greet,
    out_sem,
):
    seq, chan = lax.axis_index("seq"), lax.axis_index("chan")
    count = lax.axis_size("seq")
    half, col = lax.div(chan, 4), lax.rem(chan, 4)
    upper = half == 1
    odd = lax.rem(seq, 2) == 1
    even = jnp.logical_not(odd)
    lags = range(1, LAGS + 1)
    spans = range(LAGS + 1)

    def ahead(k):
        return (seq + k, chan)

    def across(k):
        return (seq + k, (1 - half) * 4 + col)

    def beside(shift):
        return (seq, half * 4 + lax.rem(col + shift, 4))

    row, side = lax.div(seq, 8), lax.rem(lax.div(seq, 2), 4) == 3
    hub = jnp.logical_and(side, lax.rem(row, 2) == 1)
    spoke = jnp.logical_and(side, lax.rem(row, 2) == 0)
    lower = jnp.logical_not(upper)

    def both(*conditions):
        return functools.reduce(jnp.logical_and, conditions)

    def has(k):
        return jnp.logical_and(seq + k >= 0, seq + k < count)

    def signal(sem, device):
        pl.semaphore_signal(sem, inc=1, device_id=device, device_id_type=MESH)

    loads = [
        pltpu.make_async_copy(src, dst, load_sem.at[n])
        for n, (src, dst) in enumerate(
            [
                (x_hbm, xv),
                (tab_hbm, tab),
                (taps_hbm, taps),
                (skip_hbm, skip),
                (gate_hbm, gate),
            ]
        )
    ]

    loads[0].start()
    barrier = pltpu.get_barrier_semaphore()
    @pl.when(lower)
    def _():
        for k in range(-LAGS, LAGS + 1):
            pl.when(has(k))(functools.partial(signal, barrier, across(k)))
        pl.when(hub)(functools.partial(signal, barrier, across(-8)))

        @pl.when(spoke)
        def _():
            signal(barrier, ahead(8))
            pl.when(odd)(functools.partial(signal, barrier, ahead(7)))

    for shift in (1, 2, 3):
        signal(barrier, beside(shift))
    for k in lags:
        pl.when(has(k))(functools.partial(signal, barrier, ahead(k)))

    for load in loads[1:]:
        load.start()

    loads[0].wait()
    gram = lax.dot_general(
        xv[...], xv[...], (((1,), (1,)), ((), ())), preferred_element_type=jnp.float32
    )
    diagonal = lax.broadcasted_iota(jnp.int32, (B, B), 0) == lax.broadcasted_iota(
        jnp.int32, (B, B), 1
    )
    part[...] = jnp.sum(jnp.where(diagonal, gram, 0.0), axis=0, keepdims=True)

    for k in lags:

        @pl.when(seq < k)
        def _():
            halo[k - 1] = jnp.zeros(halo.shape[1:], halo.dtype)

    for load in loads[1:4]:
        load.wait()

    def filter_spectra(step, carry):
        cols = pl.ds(pl.multiple_of(step * CW, CW), CW)
        last_re = last_im = None
        for lag in spans:
            if lag < LAGS:
                block = taps[lag * B : (lag + 1) * B, cols]
                here = jnp.dot(
                    tab[: 2 * B],
                    jnp.concatenate([block, block], 0),
                    preferred_element_type=jnp.float32,
                )
                re, im = here[:B], here[B:]
                full_re, full_im = (re + skip[:, cols] if lag == 0 else re), im
            else:
                tap = taps[LAGS * B : LAGS * B + 1, cols].astype(jnp.float32)
                full_re, full_im = jnp.broadcast_to(tap, (B, CW)), jnp.zeros((B, CW), jnp.float32)
            if last_re is not None:
                h = B // 2
                turned_re = jnp.concatenate([-last_im[:h], last_im[h:]], 0)
                turned_im = jnp.concatenate([last_re[:h], -last_re[h:]], 0)
                full_re, full_im = full_re + turned_re, full_im + turned_im
            spec[lag, :B, cols] = full_re
            spec[lag, B:, cols] = full_im
            if lag < LAGS:
                last_re, last_im = re, im
        return carry

    steps = xv.shape[1] // CW
    lax.fori_loop(0, steps, filter_spectra, 0)

    before, after = jnp.minimum(seq, LAGS), jnp.minimum(count - 1 - seq, LAGS)
    far = half * (before + after + 1 + spoke.astype(jnp.int32))
    extra = (1 - half) * hub.astype(jnp.int32) * (2 - lax.rem(seq, 2))
    pl.semaphore_wait(barrier, 3 + before + far + extra)

    @pl.when(upper)
    def _():
        for k in spans:
            pl.when(has(-k))(functools.partial(signal, greet.at[2], across(-k)))

    def remote(src, dst, send, recv, device):
        return pltpu.make_async_remote_copy(
            src_ref=src,
            dst_ref=dst,
            send_sem=send,
            recv_sem=recv,
            device_id=device,
            device_id_type=MESH,
        )

    def piece(n):
        return pl.ds(n * ROWS, ROWS)

    def to_next(src, slot, n, rows):
        return remote(
            src.at[rows],
            halo.at[slot, rows],
            next_send.at[slot // 2],
            next_recv.at[slot // 2, n],
            ahead(2),
        )

    def to_mate(src, slot, rows):
        return remote(
            src.at[rows],
            halo.at[slot, rows],
            mate_send.at[slot // 2],
            mate_recv.at[slot // 2],
            ahead(1 - 2 * lax.rem(seq, 2)),
        )

    pieces = range(CHUNKS)
    whole = pl.ds(0, B)
    own = [to_next(x_hbm, 1, n, piece(n)) for n in pieces]
    onward = [to_next(halo.at[1], 3, n, piece(n)) for n in pieces]
    even_first = to_mate(x_hbm, 0, whole)
    even_second = [to_mate(halo.at[1], 2, piece(n)) for n in pieces]
    odd_first = [to_mate(halo.at[1], 0, piece(n)) for n in pieces]
    odd_second = [to_mate(halo.at[3], 2, piece(n)) for n in pieces]
    all_next = [to_next(halo.at[slot], slot, 0, whole) for slot in (1, 3)]
    all_mate = [to_mate(halo.at[slot], slot, whole) for slot in (0, 2)]

    def gather(ref, sems, amount, most):
        def on(act):
            for n in range(1, most + 1):
                rows = ref.at[pl.ds(0, n)]
                copy = remote(rows, rows, sems.at[0], sems.at[1], beside(1))
                pl.when(amount == n)(functools.partial(act, copy))

        return on

    def each(copies, act):
        for copy in copies:
            act(copy)

    xs = [
        remote(part, xpart.at[d - 1], x_sem.at[0], x_sem.at[1], beside(d))
        for d in (1, 2, 3)
    ]
    each(xs, lambda copy: copy.start())

    for k in (2, 1, 3, 4):
        pl.when(has(-k))(functools.partial(signal, greet.at[(k - 1) // 2], ahead(-k)))

    every_x = remote(xpart, xpart, x_sem.at[0], x_sem.at[1], beside(1))

    pl.when(has(1))(lambda: pl.semaphore_wait(greet.at[0], jnp.minimum(after, 2)))
    pl.when(has(2))(lambda: each(own, lambda copy: copy.start()))
    pl.when(even)(lambda: even_first.start())
    every_x.wait_recv()
    xsum[...] = part[...] + xpart[0] + xpart[1] + xpart[2]
    nears = [
        remote(xsum, near.at[k - 1], near_sem.at[0], near_sem.at[1], ahead(k))
        for k in lags
    ]
    aways = [
        remote(xsum, away.at[k], away_sem.at[0], away_sem.at[1], across(k)) for k in spans
    ]

    def direct(k):
        if k > 1:
            return has(k)
        handed = both(upper, spoke) if k == 0 else both(upper, spoke, even)
        return both(has(k), jnp.logical_not(handed))

    to_hub = remote(xsum, handed_sum.at[0], away_sem.at[0], hub_sem.at[1], across(8))
    from_hub = [
        remote(handed_sum.at[0], away.at[k], hub_sem.at[0], away_sem.at[1], ahead(k - 8))
        for k in (0, 1)
    ]

    def send_away():
        pl.when(both(upper, spoke))(lambda: to_hub.start())
        for k in spans:
            pl.when(direct(k))(lambda copy=aways[k]: copy.start())

    pl.when(upper)(send_away)
    pl.when(has(3))(lambda: pl.semaphore_wait(greet.at[1], after - 2))
    for k in lags:
        pl.when(has(k))(lambda copy=nears[k - 1]: copy.start())

    @pl.when(has(-2))
    def _():
        for n in pieces:
            own[n].wait_recv()
            pl.when(has(2))(lambda n=n: onward[n].start())
            pl.when(odd)(lambda n=n: odd_first[n].start())
            pl.when(even)(lambda n=n: even_second[n].start())

    @pl.when(jnp.logical_not(upper))
    def _():
        pl.semaphore_wait(greet.at[2], after + 1)
        send_away()

        @pl.when(hub)
        def _():
            to_hub.wait_recv()
            from_hub[0].start()
            pl.when(even)(lambda: from_hub[1].start())

    @pl.when(has(-4))
    def _():
        for n in pieces:
            onward[n].wait_recv()
            pl.when(odd)(lambda n=n: odd_second[n].start())

    each(loads[4:], lambda copy: copy.wait())

    def scaled(lag):
        if lag == 0:
            sums = xsum[...] + away[0]
        else:
            sums = near[lag - 1] + away[lag]
        scale = lax.rsqrt(sums * (1.0 / D) + 1e-06)
        if lag:
            scale = jnp.where(seq >= lag, scale, 0.0)
        hi, lo = split((tab[: 2 * B, :B].astype(jnp.float32) + tab[: 2 * B, B:].astype(jnp.float32)) * scale)
        fs[lag, :, :B] = hi
        fs[lag, :, B:] = lo

    def leave(step):
        cols = pl.ds(pl.multiple_of(step * WIDE, WIDE), WIDE)
        return pltpu.make_async_copy(out.at[:, cols], out_hbm.at[:, cols], out_sem)

    def sent(*copies):
        each(copies, lambda copy: copy.wait_send())

    every_x.wait_send()
    gather(near, near_sem, after, LAGS)(lambda copy: copy.wait_send())
    pl.when(has(2))(lambda: sent(all_next[0]))
    pl.when(both(has(2), has(-2)))(lambda: sent(all_next[1]))
    pl.when(jnp.logical_or(even, has(-2)))(lambda: sent(all_mate[0]))
    pl.when(jnp.logical_or(both(even, has(-2)), has(-4)))(lambda: sent(all_mate[1]))
    pl.when(has(-1))(lambda: all_mate[0].wait_recv())
    pl.when(has(-3))(lambda: all_mate[1].wait_recv())
    gather(near, near_sem, before, LAGS)(lambda copy: copy.wait_recv())
    gather(away, away_sem, before + 1, LAGS + 1)(lambda copy: copy.wait_recv())
    for lag in spans:
        scaled(lag)

    def convolve(step, carry):
        cols = pl.ds(pl.multiple_of(step * WIDE, WIDE), WIDE)
        acc_re = acc_im = None
        for lag in spans:
            block = xv[:, cols] if lag == 0 else halo[lag - 1, :, cols]
            here = jnp.dot(
                fs[lag], jnp.concatenate([block, block], 0), preferred_element_type=jnp.float32
            )
            re, im = here[:B], here[B:]
            sre, sim = spec[lag, :B, cols], spec[lag, B:, cols]
            new_re, new_im = re * sre - im * sim, re * sim + im * sre
            acc_re = new_re if lag == 0 else acc_re + new_re
            acc_im = new_im if lag == 0 else acc_im + new_im
        hi, lo = split(jnp.concatenate([acc_re, acc_im], 0))
        ihi, ilo = tab[2 * B : 3 * B], tab[3 * B :]
        result = (
            jnp.dot(ihi, hi, preferred_element_type=jnp.float32)
            + jnp.dot(ihi, lo, preferred_element_type=jnp.float32)
            + jnp.dot(ilo, hi, preferred_element_type=jnp.float32)
        )
        out[:, cols] = (gate[:, cols].astype(jnp.float32) * result).astype(jnp.bfloat16)
        leave(step).start()
        return carry

    wides = xv.shape[1] // WIDE
    lax.fori_loop(0, wides, convolve, 0)

    left = after + 1 - both(upper, spoke, even).astype(jnp.int32)
    gather(away, away_sem, left, LAGS + 1)(lambda copy: copy.wait_send())
    handed_on = both(lower, hub).astype(jnp.int32) * (2 - lax.rem(seq, 2))
    gather(handed_sum, hub_sem, handed_on, 2)(lambda copy: copy.wait_send())
    pltpu.make_async_copy(out, out_hbm, out_sem).wait()


def on_device(inputs, gating, long_filter, skip_scale):
    rows, channels = inputs.shape
    bf16, f32 = jnp.bfloat16, jnp.float32
    tab = tables()
    dma = pltpu.SemaphoreType.DMA
    return pl.pallas_call(
        kernel,
        out_shape=jax.ShapeDtypeStruct((rows, channels), bf16),
        in_specs=[pl.BlockSpec(memory_space=pltpu.HBM)] * 5,
        out_specs=pl.BlockSpec(memory_space=pl.ANY),
        scratch_shapes=[
            pltpu.VMEM((rows, channels), bf16),
            pltpu.VMEM((rows, channels), bf16),
            pltpu.VMEM(long_filter.shape, bf16),
            pltpu.VMEM((1, channels), f32),
            pltpu.VMEM(tab.shape, bf16),
            pltpu.VMEM((LAGS, rows, channels), bf16),
            pltpu.VMEM((LAGS + 1, 2 * B, channels), f32),
            pltpu.VMEM((LAGS + 1, 2 * B, 2 * B), bf16),
            pltpu.VMEM((rows, channels), bf16),
            pltpu.VMEM((1, B), f32),
            pltpu.VMEM((3, 1, B), f32),
            pltpu.VMEM((1, B), f32),
            pltpu.VMEM((LAGS, 1, B), f32),
            pltpu.VMEM((LAGS + 1, 1, B), f32),
            pltpu.VMEM((2, 1, B), f32),
            dma((5,)),
            dma((2,)),
            dma((2,)),
            dma((2, CHUNKS)),
            dma((2,)),
            dma((2,)),
            dma((2,)),
            dma((2,)),
            dma((2,)),
            pltpu.SemaphoreType.REGULAR((3,)),
            dma,
        ],
        compiler_params=pltpu.CompilerParams(
            collective_id=0, has_side_effects=True, vmem_limit_bytes=60 * 1024 * 1024
        ),
    )(inputs, gating, long_filter, skip_scale[None, :], tab)


def solution(mesh):
    in_specs = (P("seq", "chan"), P("seq", "chan"), P(None, "chan"), P("chan"))
    return jax.shard_map(
        on_device, mesh=mesh, in_specs=in_specs, out_specs=P("seq", "chan"), check_vma=False
    )
```

```python
import functools

import jax
import jax.numpy as jnp
import numpy as np
from jax import lax
from jax.experimental import pallas as pl
from jax.experimental.pallas import tpu as pltpu
from jax.sharding import PartitionSpec as P

D = 8192
MESH = pl.DeviceIdType.MESH
B = 128
LAGS = 4
CW = 256
WIDE = 512
CHUNKS = 4
ROWS = B // CHUNKS


def split(value):
    hi = value.astype(jnp.bfloat16)
    return hi, (value - hi.astype(jnp.float32)).astype(jnp.bfloat16)


def tables():
    bins = np.concatenate([np.arange(0, B, 2), np.arange(1, B, 2)])
    angle = np.pi * np.outer(2 * bins + 1, np.arange(B)) / (2 * B)
    forward = np.concatenate([np.cos(angle), -np.sin(angle)], 0)
    inverse = forward.T / B

    def halves(table):
        table = table.astype(np.float32)
        hi = table.astype(jnp.bfloat16)
        return [hi, (table - hi.astype(np.float32)).astype(jnp.bfloat16)]

    return np.concatenate([np.concatenate(halves(forward), 1)] + halves(inverse), 0)


def kernel(
    x_hbm,
    gate_hbm,
    taps_hbm,
    skip_hbm,
    tab_hbm,
    out_hbm,
    xv,
    gate,
    taps,
    skip,
    tab,
    halo,
    spec,
    fs,
    out,
    part,
    xpart,
    xsum,
    near,
    away,
    handed_sum,
    load_sem,
    next_send,
    mate_send,
    next_recv,
    mate_recv,
    x_sem,
    near_sem,
    away_sem,
    hub_sem,
    greet,
    out_sem,
):
    seq, chan = lax.axis_index("seq"), lax.axis_index("chan")
    count = lax.axis_size("seq")
    half, col = lax.div(chan, 4), lax.rem(chan, 4)
    upper = half == 1
    odd = lax.rem(seq, 2) == 1
    even = jnp.logical_not(odd)
    lags = range(1, LAGS + 1)
    spans = range(LAGS + 1)

    def ahead(k):
        return (seq + k, chan)

    def across(k):
        return (seq + k, (1 - half) * 4 + col)

    def beside(shift):
        return (seq, half * 4 + lax.rem(col + shift, 4))

    row, side = lax.div(seq, 8), lax.rem(lax.div(seq, 2), 4) == 3
    hub = jnp.logical_and(side, lax.rem(row, 2) == 1)
    spoke = jnp.logical_and(side, lax.rem(row, 2) == 0)
    lower = jnp.logical_not(upper)

    def both(*conditions):
        return functools.reduce(jnp.logical_and, conditions)

    def has(k):
        return jnp.logical_and(seq + k >= 0, seq + k < count)

    def signal(sem, device):
        pl.semaphore_signal(sem, inc=1, device_id=device, device_id_type=MESH)

    loads = [
        pltpu.make_async_copy(src, dst, load_sem.at[n])
        for n, (src, dst) in enumerate(
            [
                (x_hbm, xv),
                (tab_hbm, tab),
                (taps_hbm, taps),
                (skip_hbm, skip),
                (gate_hbm, gate),
            ]
        )
    ]

    loads[0].start()
    barrier = pltpu.get_barrier_semaphore()
    @pl.when(lower)
    def _():
        for k in range(-LAGS, LAGS + 1):
            pl.when(has(k))(functools.partial(signal, barrier, across(k)))
        pl.when(hub)(functools.partial(signal, barrier, across(-8)))

        @pl.when(spoke)
        def _():
            signal(barrier, ahead(8))
            pl.when(odd)(functools.partial(signal, barrier, ahead(7)))

    for shift in (1, 2, 3):
        signal(barrier, beside(shift))
    for k in lags:
        pl.when(has(k))(functools.partial(signal, barrier, ahead(k)))

    for load in loads[1:]:
        load.start()

    loads[0].wait()
    gram = lax.dot_general(
        xv[...], xv[...], (((1,), (1,)), ((), ())), preferred_element_type=jnp.float32
    )
    diagonal = lax.broadcasted_iota(jnp.int32, (B, B), 0) == lax.broadcasted_iota(
        jnp.int32, (B, B), 1
    )
    part[...] = jnp.sum(jnp.where(diagonal, gram, 0.0), axis=0, keepdims=True)

    before, after = jnp.minimum(seq, LAGS), jnp.minimum(count - 1 - seq, LAGS)
    far = half * (before + after + 1 + spoke.astype(jnp.int32))
    extra = (1 - half) * hub.astype(jnp.int32) * (2 - lax.rem(seq, 2))
    pl.semaphore_wait(barrier, 3 + before + far + extra)

    @pl.when(upper)
    def _():
        for k in spans:
            pl.when(has(-k))(functools.partial(signal, greet.at[2], across(-k)))

    def remote(src, dst, send, recv, device):
        return pltpu.make_async_remote_copy(
            src_ref=src,
            dst_ref=dst,
            send_sem=send,
            recv_sem=recv,
            device_id=device,
            device_id_type=MESH,
        )

    def piece(n):
        return pl.ds(n * ROWS, ROWS)

    def to_next(src, slot, n, rows):
        return remote(
            src.at[rows],
            halo.at[slot, rows],
            next_send.at[slot // 2],
            next_recv.at[slot // 2, n],
            ahead(2),
        )

    def to_mate(src, slot, rows):
        return remote(
            src.at[rows],
            halo.at[slot, rows],
            mate_send.at[slot // 2],
            mate_recv.at[slot // 2],
            ahead(1 - 2 * lax.rem(seq, 2)),
        )

    pieces = range(CHUNKS)
    whole = pl.ds(0, B)
    own = [to_next(x_hbm, 1, n, piece(n)) for n in pieces]
    onward = [to_next(halo.at[1], 3, n, piece(n)) for n in pieces]
    even_first = to_mate(x_hbm, 0, whole)
    even_second = [to_mate(halo.at[1], 2, piece(n)) for n in pieces]
    odd_first = [to_mate(halo.at[1], 0, piece(n)) for n in pieces]
    odd_second = [to_mate(halo.at[3], 2, piece(n)) for n in pieces]
    all_next = [to_next(halo.at[slot], slot, 0, whole) for slot in (1, 3)]
    all_mate = [to_mate(halo.at[slot], slot, whole) for slot in (0, 2)]

    def gather(ref, sems, amount, most):
        def on(act):
            for n in range(1, most + 1):
                rows = ref.at[pl.ds(0, n)]
                copy = remote(rows, rows, sems.at[0], sems.at[1], beside(1))
                pl.when(amount == n)(functools.partial(act, copy))

        return on

    def each(copies, act):
        for copy in copies:
            act(copy)

    xs = [
        remote(part, xpart.at[d - 1], x_sem.at[0], x_sem.at[1], beside(d))
        for d in (1, 2, 3)
    ]
    each(xs, lambda copy: copy.start())

    for k in (2, 1, 3, 4):
        pl.when(has(-k))(functools.partial(signal, greet.at[(k - 1) // 2], ahead(-k)))

    pl.when(has(1))(lambda: pl.semaphore_wait(greet.at[0], jnp.minimum(after, 2)))
    pl.when(has(2))(lambda: each(own, lambda copy: copy.start()))
    pl.when(even)(lambda: even_first.start())

    for k in lags:

        @pl.when(seq < k)
        def _():
            halo[k - 1] = jnp.zeros(halo.shape[1:], halo.dtype)

    every_x = remote(xpart, xpart, x_sem.at[0], x_sem.at[1], beside(1))

    each(loads[1:4], lambda copy: copy.wait())

    def filter_spectra(step, carry):
        cols = pl.ds(pl.multiple_of(step * CW, CW), CW)
        last_re = last_im = None
        for lag in spans:
            if lag < LAGS:
                block = taps[lag * B : (lag + 1) * B, cols]
                here = jnp.dot(
                    tab[: 2 * B],
                    jnp.concatenate([block, block], 0),
                    preferred_element_type=jnp.float32,
                )
                re, im = here[:B], here[B:]
                full_re, full_im = (re + skip[:, cols] if lag == 0 else re), im
            else:
                tap = taps[LAGS * B : LAGS * B + 1, cols].astype(jnp.float32)
                full_re, full_im = jnp.broadcast_to(tap, (B, CW)), jnp.zeros((B, CW), jnp.float32)
            if last_re is not None:
                h = B // 2
                turned_re = jnp.concatenate([-last_im[:h], last_im[h:]], 0)
                turned_im = jnp.concatenate([last_re[:h], -last_re[h:]], 0)
                full_re, full_im = full_re + turned_re, full_im + turned_im
            spec[lag, :B, cols] = full_re
            spec[lag, B:, cols] = full_im
            if lag < LAGS:
                last_re, last_im = re, im
        return carry

    steps = xv.shape[1] // CW
    lax.fori_loop(0, steps, filter_spectra, 0)

    every_x.wait_recv()
    xsum[...] = part[...] + xpart[0] + xpart[1] + xpart[2]
    nears = [
        remote(xsum, near.at[k - 1], near_sem.at[0], near_sem.at[1], ahead(k))
        for k in lags
    ]
    aways = [
        remote(xsum, away.at[k], away_sem.at[0], away_sem.at[1], across(k)) for k in spans
    ]

    def direct(k):
        if k > 1:
            return has(k)
        handed = both(upper, spoke) if k == 0 else both(upper, spoke, even)
        return both(has(k), jnp.logical_not(handed))

    to_hub = remote(xsum, handed_sum.at[0], away_sem.at[0], hub_sem.at[1], across(8))
    from_hub = [
        remote(handed_sum.at[0], away.at[k], hub_sem.at[0], away_sem.at[1], ahead(k - 8))
        for k in (0, 1)
    ]

    def send_away():
        pl.when(both(upper, spoke))(lambda: to_hub.start())
        for k in spans:
            pl.when(direct(k))(lambda copy=aways[k]: copy.start())

    pl.when(upper)(send_away)
    pl.when(has(3))(lambda: pl.semaphore_wait(greet.at[1], after - 2))
    for k in lags:
        pl.when(has(k))(lambda copy=nears[k - 1]: copy.start())

    @pl.when(has(-2))
    def _():
        for n in pieces:
            own[n].wait_recv()
            pl.when(has(2))(lambda n=n: onward[n].start())
            pl.when(odd)(lambda n=n: odd_first[n].start())
            pl.when(even)(lambda n=n: even_second[n].start())

    @pl.when(jnp.logical_not(upper))
    def _():
        pl.semaphore_wait(greet.at[2], after + 1)
        send_away()

        @pl.when(hub)
        def _():
            to_hub.wait_recv()
            from_hub[0].start()
            pl.when(even)(lambda: from_hub[1].start())

    @pl.when(has(-4))
    def _():
        for n in pieces:
            onward[n].wait_recv()
            pl.when(odd)(lambda n=n: odd_second[n].start())

    each(loads[4:], lambda copy: copy.wait())

    def scaled(lag):
        if lag == 0:
            sums = xsum[...] + away[0]
        else:
            sums = near[lag - 1] + away[lag]
        scale = lax.rsqrt(sums * (1.0 / D) + 1e-06)
        if lag:
            scale = jnp.where(seq >= lag, scale, 0.0)
        hi, lo = split((tab[: 2 * B, :B].astype(jnp.float32) + tab[: 2 * B, B:].astype(jnp.float32)) * scale)
        fs[lag, :, :B] = hi
        fs[lag, :, B:] = lo

    def leave(step):
        cols = pl.ds(pl.multiple_of(step * WIDE, WIDE), WIDE)
        return pltpu.make_async_copy(out.at[:, cols], out_hbm.at[:, cols], out_sem)

    def sent(*copies):
        each(copies, lambda copy: copy.wait_send())

    every_x.wait_send()
    gather(near, near_sem, after, LAGS)(lambda copy: copy.wait_send())
    pl.when(has(-1))(lambda: all_mate[0].wait_recv())
    pl.when(has(-3))(lambda: all_mate[1].wait_recv())
    gather(near, near_sem, before, LAGS)(lambda copy: copy.wait_recv())
    gather(away, away_sem, before + 1, LAGS + 1)(lambda copy: copy.wait_recv())
    for lag in spans:
        scaled(lag)

    def convolve(step, carry):
        cols = pl.ds(pl.multiple_of(step * WIDE, WIDE), WIDE)
        acc_re = acc_im = None
        for lag in spans:
            block = xv[:, cols] if lag == 0 else halo[lag - 1, :, cols]
            here = jnp.dot(
                fs[lag], jnp.concatenate([block, block], 0), preferred_element_type=jnp.float32
            )
            re, im = here[:B], here[B:]
            sre, sim = spec[lag, :B, cols], spec[lag, B:, cols]
            new_re, new_im = re * sre - im * sim, re * sim + im * sre
            acc_re = new_re if lag == 0 else acc_re + new_re
            acc_im = new_im if lag == 0 else acc_im + new_im
        hi, lo = split(jnp.concatenate([acc_re, acc_im], 0))
        ihi, ilo = tab[2 * B : 3 * B], tab[3 * B :]
        result = (
            jnp.dot(ihi, hi, preferred_element_type=jnp.float32)
            + jnp.dot(ihi, lo, preferred_element_type=jnp.float32)
            + jnp.dot(ilo, hi, preferred_element_type=jnp.float32)
        )
        out[:, cols] = (gate[:, cols].astype(jnp.float32) * result).astype(jnp.bfloat16)
        leave(step).start()
        return carry

    wides = xv.shape[1] // WIDE
    lax.fori_loop(0, wides, convolve, 0)

    pl.when(has(2))(lambda: sent(all_next[0]))
    pl.when(both(has(2), has(-2)))(lambda: sent(all_next[1]))
    pl.when(jnp.logical_or(even, has(-2)))(lambda: sent(all_mate[0]))
    pl.when(jnp.logical_or(both(even, has(-2)), has(-4)))(lambda: sent(all_mate[1]))
    left = after + 1 - both(upper, spoke, even).astype(jnp.int32)
    gather(away, away_sem, left, LAGS + 1)(lambda copy: copy.wait_send())
    handed_on = both(lower, hub).astype(jnp.int32) * (2 - lax.rem(seq, 2))
    gather(handed_sum, hub_sem, handed_on, 2)(lambda copy: copy.wait_send())
    pltpu.make_async_copy(out, out_hbm, out_sem).wait()


def on_device(inputs, gating, long_filter, skip_scale):
    rows, channels = inputs.shape
    bf16, f32 = jnp.bfloat16, jnp.float32
    tab = tables()
    dma = pltpu.SemaphoreType.DMA
    return pl.pallas_call(
        kernel,
        out_shape=jax.ShapeDtypeStruct((rows, channels), bf16),
        in_specs=[pl.BlockSpec(memory_space=pltpu.HBM)] * 5,
        out_specs=pl.BlockSpec(memory_space=pl.ANY),
        scratch_shapes=[
            pltpu.VMEM((rows, channels), bf16),
            pltpu.VMEM((rows, channels), bf16),
            pltpu.VMEM(long_filter.shape, bf16),
            pltpu.VMEM((1, channels), f32),
            pltpu.VMEM(tab.shape, bf16),
            pltpu.VMEM((LAGS, rows, channels), bf16),
            pltpu.VMEM((LAGS + 1, 2 * B, channels), f32),
            pltpu.VMEM((LAGS + 1, 2 * B, 2 * B), bf16),
            pltpu.VMEM((rows, channels), bf16),
            pltpu.VMEM((1, B), f32),
            pltpu.VMEM((3, 1, B), f32),
            pltpu.VMEM((1, B), f32),
            pltpu.VMEM((LAGS, 1, B), f32),
            pltpu.VMEM((LAGS + 1, 1, B), f32),
            pltpu.VMEM((2, 1, B), f32),
            dma((5,)),
            dma((2,)),
            dma((2,)),
            dma((2, CHUNKS)),
            dma((2,)),
            dma((2,)),
            dma((2,)),
            dma((2,)),
            dma((2,)),
            pltpu.SemaphoreType.REGULAR((3,)),
            dma,
        ],
        compiler_params=pltpu.CompilerParams(
            collective_id=0, has_side_effects=True, vmem_limit_bytes=60 * 1024 * 1024
        ),
    )(inputs, gating, long_filter, skip_scale[None, :], tab)


def solution(mesh):
    in_specs = (P("seq", "chan"), P("seq", "chan"), P(None, "chan"), P("chan"))
    return jax.shard_map(
        on_device, mesh=mesh, in_specs=in_specs, out_specs=P("seq", "chan"), check_vma=False
    )
```

```python
import functools

import jax
import jax.numpy as jnp
import numpy as np
from jax import lax
from jax.experimental import pallas as pl
from jax.experimental.pallas import tpu as pltpu
from jax.sharding import PartitionSpec as P

D = 8192
MESH = pl.DeviceIdType.MESH
B = 128
LAGS = 4
CW = 256
WIDE = 512
CHUNKS = 8
ROWS = B // CHUNKS


def split(value):
    hi = value.astype(jnp.bfloat16)
    return hi, (value - hi.astype(jnp.float32)).astype(jnp.bfloat16)


def tables():
    bins = np.concatenate([np.arange(0, B, 2), np.arange(1, B, 2)])
    angle = np.pi * np.outer(2 * bins + 1, np.arange(B)) / (2 * B)
    forward = np.concatenate([np.cos(angle), -np.sin(angle)], 0)
    inverse = forward.T / B

    def halves(table):
        table = table.astype(np.float32)
        hi = table.astype(jnp.bfloat16)
        return [hi, (table - hi.astype(np.float32)).astype(jnp.bfloat16)]

    return np.concatenate([np.concatenate(halves(forward), 1)] + halves(inverse), 0)


def kernel(
    x_hbm,
    gate_hbm,
    taps_hbm,
    skip_hbm,
    tab_hbm,
    out_hbm,
    xv,
    gate,
    taps,
    skip,
    tab,
    halo,
    spec,
    fs,
    out,
    part,
    xpart,
    xsum,
    near,
    away,
    handed_sum,
    load_sem,
    next_send,
    mate_send,
    next_recv,
    mate_recv,
    x_sem,
    near_sem,
    away_sem,
    hub_sem,
    greet,
    out_sem,
):
    seq, chan = lax.axis_index("seq"), lax.axis_index("chan")
    count = lax.axis_size("seq")
    half, col = lax.div(chan, 4), lax.rem(chan, 4)
    upper = half == 1
    odd = lax.rem(seq, 2) == 1
    even = jnp.logical_not(odd)
    lags = range(1, LAGS + 1)
    spans = range(LAGS + 1)

    def ahead(k):
        return (seq + k, chan)

    def across(k):
        return (seq + k, (1 - half) * 4 + col)

    def beside(shift):
        return (seq, half * 4 + lax.rem(col + shift, 4))

    row, side = lax.div(seq, 8), lax.rem(lax.div(seq, 2), 4) == 3
    hub = jnp.logical_and(side, lax.rem(row, 2) == 1)
    spoke = jnp.logical_and(side, lax.rem(row, 2) == 0)
    lower = jnp.logical_not(upper)

    def both(*conditions):
        return functools.reduce(jnp.logical_and, conditions)

    def has(k):
        return jnp.logical_and(seq + k >= 0, seq + k < count)

    def signal(sem, device):
        pl.semaphore_signal(sem, inc=1, device_id=device, device_id_type=MESH)

    loads = [
        pltpu.make_async_copy(src, dst, load_sem.at[n])
        for n, (src, dst) in enumerate(
            [
                (x_hbm, xv),
                (tab_hbm, tab),
                (taps_hbm, taps),
                (skip_hbm, skip),
                (gate_hbm, gate),
            ]
        )
    ]

    loads[0].start()
    barrier = pltpu.get_barrier_semaphore()
    @pl.when(lower)
    def _():
        for k in range(-LAGS, LAGS + 1):
            pl.when(has(k))(functools.partial(signal, barrier, across(k)))
        pl.when(hub)(functools.partial(signal, barrier, across(-8)))

        @pl.when(spoke)
        def _():
            signal(barrier, ahead(8))
            pl.when(odd)(functools.partial(signal, barrier, ahead(7)))

    for shift in (1, 2, 3):
        signal(barrier, beside(shift))
    for k in lags:
        pl.when(has(k))(functools.partial(signal, barrier, ahead(k)))

    for load in loads[1:]:
        load.start()

    loads[0].wait()
    gram = lax.dot_general(
        xv[...], xv[...], (((1,), (1,)), ((), ())), preferred_element_type=jnp.float32
    )
    diagonal = lax.broadcasted_iota(jnp.int32, (B, B), 0) == lax.broadcasted_iota(
        jnp.int32, (B, B), 1
    )
    part[...] = jnp.sum(jnp.where(diagonal, gram, 0.0), axis=0, keepdims=True)

    before, after = jnp.minimum(seq, LAGS), jnp.minimum(count - 1 - seq, LAGS)
    far = half * (before + after + 1 + spoke.astype(jnp.int32))
    extra = (1 - half) * hub.astype(jnp.int32) * (2 - lax.rem(seq, 2))
    pl.semaphore_wait(barrier, 3 + before + far + extra)

    @pl.when(upper)
    def _():
        for k in spans:
            pl.when(has(-k))(functools.partial(signal, greet.at[2], across(-k)))

    def remote(src, dst, send, recv, device):
        return pltpu.make_async_remote_copy(
            src_ref=src,
            dst_ref=dst,
            send_sem=send,
            recv_sem=recv,
            device_id=device,
            device_id_type=MESH,
        )

    def piece(n):
        return pl.ds(n * ROWS, ROWS)

    def to_next(src, slot, n, rows):
        return remote(
            src.at[rows],
            halo.at[slot, rows],
            next_send.at[slot // 2],
            next_recv.at[slot // 2, n],
            ahead(2),
        )

    def to_mate(src, slot, rows):
        return remote(
            src.at[rows],
            halo.at[slot, rows],
            mate_send.at[slot // 2],
            mate_recv.at[slot // 2],
            ahead(1 - 2 * lax.rem(seq, 2)),
        )

    pieces = range(CHUNKS)
    whole = pl.ds(0, B)
    own = [to_next(x_hbm, 1, n, piece(n)) for n in pieces]
    onward = [to_next(halo.at[1], 3, n, piece(n)) for n in pieces]
    even_first = to_mate(x_hbm, 0, whole)
    even_second = [to_mate(halo.at[1], 2, piece(n)) for n in pieces]
    odd_first = [to_mate(halo.at[1], 0, piece(n)) for n in pieces]
    odd_second = [to_mate(halo.at[3], 2, piece(n)) for n in pieces]
    all_next = [to_next(halo.at[slot], slot, 0, whole) for slot in (1, 3)]
    all_mate = [to_mate(halo.at[slot], slot, whole) for slot in (0, 2)]

    def gather(ref, sems, amount, most):
        def on(act):
            for n in range(1, most + 1):
                rows = ref.at[pl.ds(0, n)]
                copy = remote(rows, rows, sems.at[0], sems.at[1], beside(1))
                pl.when(amount == n)(functools.partial(act, copy))

        return on

    def each(copies, act):
        for copy in copies:
            act(copy)

    xs = [
        remote(part, xpart.at[d - 1], x_sem.at[0], x_sem.at[1], beside(d))
        for d in (1, 2, 3)
    ]
    each(xs, lambda copy: copy.start())

    for k in (2, 1, 3, 4):
        pl.when(has(-k))(functools.partial(signal, greet.at[(k - 1) // 2], ahead(-k)))

    pl.when(has(1))(lambda: pl.semaphore_wait(greet.at[0], jnp.minimum(after, 2)))
    pl.when(has(2))(lambda: each(own, lambda copy: copy.start()))
    pl.when(even)(lambda: even_first.start())

    for k in lags:

        @pl.when(seq < k)
        def _():
            halo[k - 1] = jnp.zeros(halo.shape[1:], halo.dtype)

    every_x = remote(xpart, xpart, x_sem.at[0], x_sem.at[1], beside(1))

    each(loads[1:4], lambda copy: copy.wait())

    def filter_spectra(step, carry):
        cols = pl.ds(pl.multiple_of(step * CW, CW), CW)
        last_re = last_im = None
        for lag in spans:
            if lag < LAGS:
                block = taps[lag * B : (lag + 1) * B, cols]
                here = jnp.dot(
                    tab[: 2 * B],
                    jnp.concatenate([block, block], 0),
                    preferred_element_type=jnp.float32,
                )
                re, im = here[:B], here[B:]
                full_re, full_im = (re + skip[:, cols] if lag == 0 else re), im
            else:
                tap = taps[LAGS * B : LAGS * B + 1, cols].astype(jnp.float32)
                full_re, full_im = jnp.broadcast_to(tap, (B, CW)), jnp.zeros((B, CW), jnp.float32)
            if last_re is not None:
                h = B // 2
                turned_re = jnp.concatenate([-last_im[:h], last_im[h:]], 0)
                turned_im = jnp.concatenate([last_re[:h], -last_re[h:]], 0)
                full_re, full_im = full_re + turned_re, full_im + turned_im
            spec[lag, :B, cols] = full_re
            spec[lag, B:, cols] = full_im
            if lag < LAGS:
                last_re, last_im = re, im
        return carry

    steps = xv.shape[1] // CW
    lax.fori_loop(0, steps, filter_spectra, 0)

    every_x.wait_recv()
    xsum[...] = part[...] + xpart[0] + xpart[1] + xpart[2]
    nears = [
        remote(xsum, near.at[k - 1], near_sem.at[0], near_sem.at[1], ahead(k))
        for k in lags
    ]
    aways = [
        remote(xsum, away.at[k], away_sem.at[0], away_sem.at[1], across(k)) for k in spans
    ]

    def direct(k):
        if k > 1:
            return has(k)
        handed = both(upper, spoke) if k == 0 else both(upper, spoke, even)
        return both(has(k), jnp.logical_not(handed))

    to_hub = remote(xsum, handed_sum.at[0], away_sem.at[0], hub_sem.at[1], across(8))
    from_hub = [
        remote(handed_sum.at[0], away.at[k], hub_sem.at[0], away_sem.at[1], ahead(k - 8))
        for k in (0, 1)
    ]

    def send_away():
        pl.when(both(upper, spoke))(lambda: to_hub.start())
        for k in spans:
            pl.when(direct(k))(lambda copy=aways[k]: copy.start())

    pl.when(upper)(send_away)
    pl.when(has(3))(lambda: pl.semaphore_wait(greet.at[1], after - 2))
    for k in lags:
        pl.when(has(k))(lambda copy=nears[k - 1]: copy.start())

    @pl.when(has(-2))
    def _():
        for n in pieces:
            own[n].wait_recv()
            pl.when(has(2))(lambda n=n: onward[n].start())
            pl.when(odd)(lambda n=n: odd_first[n].start())
            pl.when(even)(lambda n=n: even_second[n].start())

    @pl.when(jnp.logical_not(upper))
    def _():
        pl.semaphore_wait(greet.at[2], after + 1)
        send_away()

        @pl.when(hub)
        def _():
            to_hub.wait_recv()
            from_hub[0].start()
            pl.when(even)(lambda: from_hub[1].start())

    @pl.when(has(-4))
    def _():
        for n in pieces:
            onward[n].wait_recv()
            pl.when(odd)(lambda n=n: odd_second[n].start())

    each(loads[4:], lambda copy: copy.wait())

    def scaled(lag):
        if lag == 0:
            sums = xsum[...] + away[0]
        else:
            sums = near[lag - 1] + away[lag]
        scale = lax.rsqrt(sums * (1.0 / D) + 1e-06)
        if lag:
            scale = jnp.where(seq >= lag, scale, 0.0)
        hi, lo = split((tab[: 2 * B, :B].astype(jnp.float32) + tab[: 2 * B, B:].astype(jnp.float32)) * scale)
        fs[lag, :, :B] = hi
        fs[lag, :, B:] = lo

    def leave(step):
        cols = pl.ds(pl.multiple_of(step * WIDE, WIDE), WIDE)
        return pltpu.make_async_copy(out.at[:, cols], out_hbm.at[:, cols], out_sem)

    def sent(*copies):
        each(copies, lambda copy: copy.wait_send())

    every_x.wait_send()
    gather(near, near_sem, after, LAGS)(lambda copy: copy.wait_send())
    pl.when(has(-1))(lambda: all_mate[0].wait_recv())
    pl.when(has(-3))(lambda: all_mate[1].wait_recv())
    gather(near, near_sem, before, LAGS)(lambda copy: copy.wait_recv())
    gather(away, away_sem, before + 1, LAGS + 1)(lambda copy: copy.wait_recv())
    for lag in spans:
        scaled(lag)

    def convolve(step, carry):
        cols = pl.ds(pl.multiple_of(step * WIDE, WIDE), WIDE)
        acc_re = acc_im = None
        for lag in spans:
            block = xv[:, cols] if lag == 0 else halo[lag - 1, :, cols]
            here = jnp.dot(
                fs[lag], jnp.concatenate([block, block], 0), preferred_element_type=jnp.float32
            )
            re, im = here[:B], here[B:]
            sre, sim = spec[lag, :B, cols], spec[lag, B:, cols]
            new_re, new_im = re * sre - im * sim, re * sim + im * sre
            acc_re = new_re if lag == 0 else acc_re + new_re
            acc_im = new_im if lag == 0 else acc_im + new_im
        hi, lo = split(jnp.concatenate([acc_re, acc_im], 0))
        ihi, ilo = tab[2 * B : 3 * B], tab[3 * B :]
        result = (
            jnp.dot(ihi, hi, preferred_element_type=jnp.float32)
            + jnp.dot(ihi, lo, preferred_element_type=jnp.float32)
            + jnp.dot(ilo, hi, preferred_element_type=jnp.float32)
        )
        out[:, cols] = (gate[:, cols].astype(jnp.float32) * result).astype(jnp.bfloat16)
        leave(step).start()
        return carry

    wides = xv.shape[1] // WIDE
    lax.fori_loop(0, wides, convolve, 0)

    pl.when(has(2))(lambda: sent(all_next[0]))
    pl.when(both(has(2), has(-2)))(lambda: sent(all_next[1]))
    pl.when(jnp.logical_or(even, has(-2)))(lambda: sent(all_mate[0]))
    pl.when(jnp.logical_or(both(even, has(-2)), has(-4)))(lambda: sent(all_mate[1]))
    left = after + 1 - both(upper, spoke, even).astype(jnp.int32)
    gather(away, away_sem, left, LAGS + 1)(lambda copy: copy.wait_send())
    handed_on = both(lower, hub).astype(jnp.int32) * (2 - lax.rem(seq, 2))
    gather(handed_sum, hub_sem, handed_on, 2)(lambda copy: copy.wait_send())
    pltpu.make_async_copy(out, out_hbm, out_sem).wait()


def on_device(inputs, gating, long_filter, skip_scale):
    rows, channels = inputs.shape
    bf16, f32 = jnp.bfloat16, jnp.float32
    tab = tables()
    dma = pltpu.SemaphoreType.DMA
    return pl.pallas_call(
        kernel,
        out_shape=jax.ShapeDtypeStruct((rows, channels), bf16),
        in_specs=[pl.BlockSpec(memory_space=pltpu.HBM)] * 5,
        out_specs=pl.BlockSpec(memory_space=pl.ANY),
        scratch_shapes=[
            pltpu.VMEM((rows, channels), bf16),
            pltpu.VMEM((rows, channels), bf16),
            pltpu.VMEM(long_filter.shape, bf16),
            pltpu.VMEM((1, channels), f32),
            pltpu.VMEM(tab.shape, bf16),
            pltpu.VMEM((LAGS, rows, channels), bf16),
            pltpu.VMEM((LAGS + 1, 2 * B, channels), f32),
            pltpu.VMEM((LAGS + 1, 2 * B, 2 * B), bf16),
            pltpu.VMEM((rows, channels), bf16),
            pltpu.VMEM((1, B), f32),
            pltpu.VMEM((3, 1, B), f32),
            pltpu.VMEM((1, B), f32),
            pltpu.VMEM((LAGS, 1, B), f32),
            pltpu.VMEM((LAGS + 1, 1, B), f32),
            pltpu.VMEM((2, 1, B), f32),
            dma((5,)),
            dma((2,)),
            dma((2,)),
            dma((2, CHUNKS)),
            dma((2,)),
            dma((2,)),
            dma((2,)),
            dma((2,)),
            dma((2,)),
            pltpu.SemaphoreType.REGULAR((3,)),
            dma,
        ],
        compiler_params=pltpu.CompilerParams(
            collective_id=0, has_side_effects=True, vmem_limit_bytes=60 * 1024 * 1024
        ),
    )(inputs, gating, long_filter, skip_scale[None, :], tab)


def solution(mesh):
    in_specs = (P("seq", "chan"), P("seq", "chan"), P(None, "chan"), P("chan"))
    return jax.shard_map(
        on_device, mesh=mesh, in_specs=in_specs, out_specs=P("seq", "chan"), check_vma=False
    )
```
